512 devices in a mesh: basis: 32 (over x, z), angle: 8 (over y), pol: 2 (over core).
Axes of the slice: x: 4, y: 8, z: 8, core: 2. Of those that a mesh axis runs over, the one named last changes fastest.
Arguments:
- adjoint: float32 [2, 128, 256, 2, 128], P('pol', 'angle', 'basis'), may hold values from -6 to 6
- currents: float32 [2, 128, 256, 2, 128], P('pol', 'angle', 'basis'), may hold values from -6 to 6
- radiation: float32 [2, 128, 256, 2, 128], P('pol', 'angle', 'basis'), may hold values from -6 to 6
- near_blocks: bfloat16 [256, 6, 2, 128, 128], P('basis'), may hold values from -0.15625 to 0.15625
- inverse_blocks: bfloat16 [256, 2, 128, 128], P('basis'), may hold values from -0.375 to 0.375
- col_device: int32 [256, 6], P('basis'), may hold values from 0 to 31, all different within a row; in each aligned block of 8 rows (0 to 7, 8 to 15, ...) at most 3 rows name the same one
- col_offset: int32 [256, 6], P('basis'), may hold values from 0 to 7
- box_of_block: int32 [256], P('basis'), may hold values from 0 to 127
- pair_rate: float32 [256, 6], P('basis'), may hold values from -4 to 4
Outputs:
- updated: float32 [2, 128, 256, 2, 128], P('pol', 'angle', 'basis')
- shape_grad: float32 [128], P('basis')
The draws below stay inside these ranges and needn't reach their ends.
Inputs may be any that keep to these rules, and one draw needn't show every extreme that they name: `col_device`: each row names 6 different devices; the rows of one basis device name any device at most 3 times, and in some devices' rows one device exactly 3 times.
All inputs are finite; a program needn't handle non-finite values.
Results may differ from the reference program's by a relative error of at most 0.0033.
Values sent between devices are 32-bit elements; how exact they have to be, the bound alone decides.
A program may use at most 64 MiB of HBM per device.

```python
import math
import jax
import jax.numpy as jnp
import numpy as np
from jax import lax

B = 128
K = 6
NB_DEV = 8
CAP = 3
NBLK = 256
NBOX = 128
ANGLES = 128
N_BASIS = 32


def plant(drawn, own_key, least, high):
    longest = drawn.shape.index(max(drawn.shape))
    spots = []
    for shift in (0, 1):
        where = [jax.random.randint(jax.random.fold_in(own_key, axis), (), 0, length) for axis, length in enumerate(drawn.shape)]
        where[longest] = (where[longest] + shift) % drawn.shape[longest]
        spots.append(tuple(where))
    return drawn.at[spots[0]].set(least).at[spots[1]].set(high)


def levels(rng, shape, shards, least, top_value):
    level, own = 1.0, jax.random.fold_in(rng, 6)
    for axis_at, blocks in shards:
        draws = jnp.exp(jax.random.uniform(jax.random.fold_in(own, axis_at), (blocks,), jnp.float32, least / len(shards), top_value / len(shards)))
        level = level * jnp.repeat(draws, shape[axis_at] // blocks).reshape([-1 if axis == axis_at else 1 for axis in range(len(shape))])
    return level


def deal_out(own_key, own, number, rows, amount, top, limit, lean):
    order = jax.random.permutation(own_key, amount)
    heavy_load, common = load_shares(amount, rows * top, limit, lean, True), load_shares(amount, rows * top, limit, lean, False)
    places = jnp.arange(amount)

    def named(lengths, offset_by):
        used = int((lengths > 0).sum())
        fixed = max(1, used // 4)
        shifted = fixed + (places - fixed + offset_by * (used - fixed)) % max(1, amount - fixed)
        return jnp.zeros((amount,), jnp.int32).at[order[jnp.where(places < fixed, places, shifted)]].set(jnp.asarray(lengths, jnp.int32))

    lengths = jnp.where(number % 4 == 0, named(heavy_load, number // 4), named(common, number - number // 4 - 1))
    mixed = jax.random.permutation(jax.random.fold_in(own, 3), amount)
    donor, sink = mixed[0:amount // 2 * 2:2], mixed[1:amount // 2 * 2:2]
    margin = jnp.minimum(lengths[donor] - 1, limit - lengths[sink]) // 2
    margin = jnp.where((donor == order[0]) | (sink == order[0]) | (lengths[sink] == 0), 0, jnp.maximum(margin, 0))
    shifted = jax.random.randint(jax.random.fold_in(own, 4), (amount // 2,), 0, 1 << 20) % (margin + 1)
    lengths = lengths.at[donor].add(-shifted).at[sink].add(shifted)
    items = jnp.searchsorted(jnp.cumsum(lengths), jnp.arange(rows * top), side="right").astype(jnp.int32)
    grid = items.reshape(top, rows).T
    grid = grid[jax.random.permutation(jax.random.fold_in(own, 1), rows)]
    offset_by = jax.random.randint(jax.random.fold_in(own, 2), (rows, 1), 0, top)
    return jnp.take_along_axis(grid, (jnp.arange(top)[None, :] + offset_by) % top, axis=1)


def load_shares(amount, total, bound, slope, full):
    weights = [(1 << 20) // math.isqrt(grade ** slope) + 1 for grade in range(1, amount + 1)]
    largest = bound if full else min(bound, max(-(-total // amount), total * weights[0] // sum(weights)))
    least = 1 if total - largest >= amount - 1 else 0
    holding, rest = [largest] + [least] * (amount - 1), total - largest - least * (amount - 1)
    while rest > 0:
        movable = [i for i in range(1, amount) if holding[i] < largest] or [i for i in range(1, amount) if holding[i] < bound]
        whole, left = sum([weights[i] for i in movable]), rest
        for i in movable:
            more = min(bound - holding[i], max(1, left * weights[i] // whole), rest)
            holding[i] = holding[i] + more
            rest = rest - more
    return np.array(holding)


def noise(stream_key, dims, deviation, limit, shards=(), kind=jnp.bfloat16):
    values = jax.random.normal(stream_key, dims, jnp.float32) * deviation
    if len(shards) > 0:
        values = levels(stream_key, dims, shards, -0.22, 0.18) * values
    return jnp.clip(values, min=-limit, max=limit).astype(kind)


def setup_inputs(seed: int = 0) -> dict:
    key_of = jax.random.split(jax.random.key(seed), 10)
    adjoint = noise(key_of[0], (2, ANGLES, NBLK, 2, B), 1.0, 6.0, ((0, 2), (1, 8), (2, 32)), jnp.float32)
    currents = noise(key_of[1], (2, ANGLES, NBLK, 2, B), 1.0, 6.0, ((0, 2), (1, 8), (2, 32)), jnp.float32)
    radiation = noise(key_of[2], (2, ANGLES, NBLK, 2, B), 1.0, 6.0, ((0, 2), (1, 8), (2, 32)), jnp.float32)
    near_blocks = noise(key_of[3], (NBLK, K, 2, B, B), (2 * B * K) ** -0.5, 0.15625, ((0, 32),))
    inverse_blocks = noise(key_of[4], (NBLK, 2, B, B), (2 * B) ** -0.5, 0.375, ((0, 32),))
    col_device_keys = jax.random.split(jax.random.fold_in(key_of[5], 1), NBLK // NB_DEV)
    col_device_turns = jax.random.permutation(jax.random.fold_in(key_of[5], 3), NBLK // NB_DEV)
    col_device = jax.vmap(lambda own, number: deal_out(jax.random.fold_in(key_of[5], 2), own, number, NB_DEV, N_BASIS, K, CAP, 2))(col_device_keys, col_device_turns).reshape((NBLK, K))
    col_offset = plant(jax.random.randint(key_of[6], (NBLK, K), 0, NB_DEV), jax.random.fold_in(key_of[6], 1), 0, NB_DEV - 1).astype(jnp.int32)
    box_of_block = plant(jax.random.randint(key_of[7], (NBLK,), 0, NBOX), jax.random.fold_in(key_of[7], 1), 0, NBOX - 1).astype(jnp.int32)
    pair_rate = noise(key_of[8], (NBLK, K), 1.0, 4.0, ((0, 32),), jnp.float32)
    return {"adjoint": adjoint, "currents": currents, "radiation": radiation, "near_blocks": near_blocks, "inverse_blocks": inverse_blocks, "col_device": col_device, "col_offset": col_offset, "box_of_block": box_of_block, "pair_rate": pair_rate}


def conjugate_apply(matrices, vectors):
    highest = lax.Precision.HIGHEST
    real_part = jnp.einsum('nm,...n->...m', matrices[0], vectors[..., 0, :], precision=highest) + jnp.einsum('nm,...n->...m', matrices[1], vectors[..., 1, :], precision=highest)
    imag_part = jnp.einsum('nm,...n->...m', matrices[0], vectors[..., 1, :], precision=highest) - jnp.einsum('nm,...n->...m', matrices[1], vectors[..., 0, :], precision=highest)
    return jnp.stack([real_part, imag_part], axis=-2)

def reference(adjoint, currents, radiation, near_blocks, inverse_blocks, col_device, col_offset, box_of_block, pair_rate):
    highest = lax.Precision.HIGHEST
    norm_far = 1.0 / math.sqrt(NBLK * B)
    rad_real = radiation[:, :, :, 0, :]
    rad_imag = radiation[:, :, :, 1, :]
    cur_real = currents[:, :, :, 0, :]
    cur_imag = currents[:, :, :, 1, :]
    far_real = (lax.optimization_barrier(jnp.sum(rad_real * cur_real - rad_imag * cur_imag, axis=(2, 3))) * norm_far)[:, :, None, None]
    far_imag = (lax.optimization_barrier(jnp.sum(rad_real * cur_imag + rad_imag * cur_real, axis=(2, 3))) * norm_far)[:, :, None, None]
    source = jnp.stack([far_real * rad_real + far_imag * rad_imag, far_imag * rad_real - far_real * rad_imag], axis=3)
    rounded = lax.optimization_barrier(adjoint.astype(jnp.bfloat16)).astype(jnp.float32)
    columns = (col_device * NB_DEV + col_offset).astype(jnp.int32)

    def row_step(carry, row_index):
        totals, box_sums = carry
        matrices = near_blocks[row_index].astype(jnp.float32)
        vectors = lax.dynamic_index_in_dim(rounded, row_index, axis=2, keepdims=False)
        for slot_index in range(K):
            term = conjugate_apply(matrices[slot_index], vectors)
            column = columns[row_index, slot_index]
            totals = totals.at[:, :, column].add(term)
            beside = lax.dynamic_index_in_dim(currents, column, axis=2, keepdims=False)
            box_sums = box_sums.at[box_of_block[row_index]].add(pair_rate[row_index, slot_index] * jnp.sum(term * beside))
        return ((totals, box_sums), None)
    start = (jnp.zeros(source.shape, jnp.float32), jnp.zeros((NBOX,), jnp.float32))
    (totals, box_sums), _ = lax.scan(row_step, start, jnp.arange(NBLK, dtype=jnp.int32))
    residual = lax.optimization_barrier((source - totals).astype(jnp.bfloat16)).astype(jnp.float32)
    inverse = inverse_blocks.astype(jnp.float32)
    res_real = residual[:, :, :, 0, :]
    res_imag = residual[:, :, :, 1, :]
    upd_real = jnp.einsum('cnm,pacn->pacm', inverse[:, 0], res_real, precision=highest) + jnp.einsum('cnm,pacn->pacm', inverse[:, 1], res_imag, precision=highest)
    upd_imag = jnp.einsum('cnm,pacn->pacm', inverse[:, 0], res_imag, precision=highest) - jnp.einsum('cnm,pacn->pacm', inverse[:, 1], res_real, precision=highest)
    updated = adjoint + jnp.stack([upd_real, upd_imag], axis=3)
    shape_grad = box_sums * (-1.0 / math.sqrt(4 * B * ANGLES * K))
    return (updated, shape_grad)
```

```python
import functools
import math

import jax
import jax.numpy as jnp
from jax import lax
from jax.experimental import pallas as pl
from jax.experimental.pallas import tpu as pltpu
from jax.sharding import PartitionSpec as P

MESH = pl.DeviceIdType.MESH
F32 = jnp.float32
BF16 = jnp.bfloat16

NX, NZ = 4, 8
CAP = 3
BOX_DEV = 4
ORDER = (4, 3, 5, 2, 6, 1, 7, 0)
PLACE = {distance % NZ: place for place, distance in enumerate(ORDER)}


def kernel(
    sizes,
    pair_tab,
    adj,
    cur,
    rad,
    off_tab,
    rate_box_tab,
    near_hbm,
    inv_hbm,
    out,
    grad,
    near,
    inv,
    lhs,
    sent,
    got,
    cur_at,
    part,
    part_got,
    own_sum,
    msg,
    msg_got,
    far_sum,
    far_got,
    lane_dots,
    g_sum,
    g_got,
    local_sem,
    term_s,
    term_r,
    cur_s,
    cur_r,
    part_s,
    part_r,
    msg_s,
    msg_r,
    far_s,
    far_r,
    g_s,
    g_r,
):
    ny, nc, norm_far = sizes
    blocks = 8
    b = lax.axis_index("basis")
    y = lax.axis_index("angle")
    c0 = lax.axis_index("pol")
    x = lax.div(b, NZ)
    z = lax.rem(b, NZ)

    def at(dx=0, dz=0, dy=0, dc=0):
        basis = lax.rem(x + dx, NX) * NZ + lax.rem(z + dz, NZ)
        return (basis, lax.rem(y + dy, ny), lax.rem(c0 + dc, nc))

    def remote(src, dst, send_sem, recv_sem, device):
        return pltpu.make_async_remote_copy(
            src_ref=src,
            dst_ref=dst,
            send_sem=send_sem,
            recv_sem=recv_sem,
            device_id=device,
            device_id_type=MESH,
        )

    near_copy = pltpu.make_async_copy(near_hbm, near, local_sem.at[0])
    inv_copy = pltpu.make_async_copy(inv_hbm, inv, local_sem.at[1])
    near_copy.start()
    inv_copy.start()

    xc = [(dx, dc) for dx in range(NX) for dc in range(nc) if dx or dc]
    groups = [
        [(dx * nc + dc, at(dx=dx, dc=dc)) for dx, dc in xc],
        [(dz, at(dz=dz)) for dz in range(1, NZ)],
        [(dy, at(dy=dy)) for dy in range(1, ny)],
    ]
    barrier = pltpu.get_barrier_semaphore()
    for group in groups:
        for _, device in group:
            pl.semaphore_signal(barrier, inc=1, device_id=device, device_id_type=MESH)

    far_re = jnp.zeros((16, 128), F32)
    far_im = jnp.zeros((16, 128), F32)
    for r in range(blocks):
        re = pl.ds(2 * r, 16, stride=16)
        im = pl.ds(2 * r + 1, 16, stride=16)
        ar, ai = adj[re, :].astype(BF16), adj[im, :].astype(BF16)
        lhs[r, 0:16, 0:128] = ar
        lhs[r, 0:16, 128:256] = ai
        lhs[r, 16:32, 0:128] = ai
        lhs[r, 16:32, 128:256] = -ar
        cr, ci = cur[re, :], cur[im, :]
        cur_at[PLACE[0], r, 0:2] = cr.reshape(2, 8, 128)
        cur_at[PLACE[0], r, 2:4] = ci.reshape(2, 8, 128)
        rr, ri = rad[re, :], rad[im, :]
        far_re += rr * cr - ri * ci
        far_im += rr * ci + ri * cr
    lane = lax.broadcasted_iota(jnp.int32, (16, 128), 1)
    far_tile = jnp.where(
        lane < 64,
        jnp.sum(far_re, axis=1, keepdims=True),
        jnp.sum(far_im, axis=1, keepdims=True),
    )
    for k in range(NX):
        msg[k, 0:16] = far_tile
        msg[k, 16:40] = off_tab[k]
        msg[k, 40:64] = rate_box_tab[k]
    msg_got[0] = msg[0]

    pl.semaphore_wait(barrier, sum(len(group) for group in groups))

    msgs = [
        remote(msg.at[k], msg_got.at[k], msg_s.at[k], msg_r.at[k], at(dx=k))
        for k in range(1, NX)
    ]
    for copy in msgs:
        copy.start()

    half = blocks // 2

    def cur_step(way, step):
        sign = 1 if way == 0 else -1
        have = PLACE[(-sign * (step - 1)) % NZ]
        want = PLACE[(-sign * step) % NZ]
        rows = slice(None) if step < 4 else slice(way * half, (way + 1) * half)
        return remote(
            cur_at.at[have, rows],
            cur_at.at[want, rows],
            cur_s.at[way, step - 1],
            cur_r.at[way, step - 1],
            at(dz=sign % NZ),
        )

    cur_copies = {(way, step): cur_step(way, step) for way in (0, 1) for step in range(1, 5)}

    def forward_currents(step):
        for way in (0, 1):
            cur_copies[way, step - 1].wait_recv()
            cur_copies[way, step].start()

    for way in (0, 1):
        cur_copies[way, 1].start()
    near_copy.wait()

    def term_copy(place, k):
        return remote(
            sent.at[place, k - 1],
            got.at[place, k],
            term_s.at[place, k - 1],
            term_r.at[place, k - 1],
            at(dx=k),
        )

    def send_terms(place, _):
        for k in (2, 1, 3, 0):
            for s in range(CAP):
                pair = pair_tab[k * NZ * CAP + place * CAP + s]
                term = jnp.dot(
                    lhs[lax.div(pair, 6)], near[pair], preferred_element_type=F32
                ).reshape(4, 8, 128)
                if k:
                    sent[place, k - 1, s] = term
                else:
                    got[place, 0, s] = term
            if k:
                term_copy(place, k).start()
        return 0

    lax.fori_loop(0, 2, send_terms, 0)

    for copy in msgs:
        copy.wait_recv()
    far_sum[...] = msg_got[0, 0:16] + msg_got[1, 0:16] + msg_got[2, 0:16] + msg_got[3, 0:16]
    fars = [
        remote(far_sum, far_got.at[k], far_s.at[k], far_r.at[k], at(dz=k)) for k in range(1, NZ)
    ]
    for copy in fars:
        copy.start()

    lax.fori_loop(2, 4, send_terms, 0)
    forward_currents(2)
    lax.fori_loop(4, 6, send_terms, 0)
    forward_currents(3)
    lax.fori_loop(6, 8, send_terms, 0)
    forward_currents(4)

    def masks(place, k, s):
        row = 16 + place * CAP + s
        off = jnp.broadcast_to(msg_got[k, row : row + 1, :], (8, 128))
        return [(off == float(c))[None] for c in range(blocks)]

    def combine(place):
        for k in range(1, NX):
            term_copy(place, k).wait_recv()
        sums = [jnp.zeros((4, 8, 128), F32) for _ in range(blocks)]
        for k in range(NX):
            for s in range(CAP):
                term = got[place, k, s]
                for c, mask in enumerate(masks(place, k, s)):
                    sums[c] = sums[c] + jnp.where(mask, term, 0.0)
        return sums

    def dots(place):
        for k in range(NX):
            for s in range(CAP):
                chosen = jnp.zeros((4, 8, 128), F32)
                for c, mask in enumerate(masks(place, k, s)):
                    chosen = jnp.where(mask, cur_at[place, c], chosen)
                product = jnp.sum(got[place, k, s] * chosen, axis=0)
                lane_dots[k, place * CAP + s : place * CAP + s + 1, :] = jnp.sum(
                    product, axis=0, keepdims=True
                )

    def part_copy(way, hops):
        rows = slice(None) if hops < 4 else slice(way * half, (way + 1) * half)
        return remote(
            part.at[way, hops - 1, rows],
            part_got.at[way, hops - 1, rows],
            part_s.at[way, hops - 1],
            part_r.at[way, hops - 1],
            at(dz=1 if way == 0 else NZ - 1),
        )

    part_copies = {(way, hops): part_copy(way, hops) for way in (0, 1) for hops in range(1, 5)}

    sums = combine(PLACE[4])
    for way in (0, 1):
        for c in range(way * half, (way + 1) * half):
            part[way, 3, c] = sums[c]
        part_copies[way, 4].start()
    for hops in (3, 2, 1):
        for way in (0, 1):
            sums = combine(PLACE[hops if way == 0 else NZ - hops])
            part_copies[way, hops + 1].wait_recv()
            for c in range(blocks):
                if hops < 3 or way * half <= c < (way + 1) * half:
                    sums[c] = sums[c] + part_got[way, hops, c]
                part[way, hops - 1, c] = sums[c]
            part_copies[way, hops].start()
    sums = combine(PLACE[0])
    for c in range(blocks):
        own_sum[c] = sums[c]

    for place in (7, 5, 6, 3, 4, 1, 2):
        dots(place)
    for way in (0, 1):
        cur_copies[way, 4].wait_recv()
    dots(0)

    value = jnp.zeros((8, 128), F32)
    box_lane = lax.broadcasted_iota(jnp.int32, (NZ * CAP, 128), 1).astype(F32)
    for k in range(NX):
        rate = msg_got[k, 40:64, 0:1]
        box = msg_got[k, 40:64, 64:65]
        pair_value = rate * jnp.sum(lane_dots[k], axis=1, keepdims=True)
        table = jnp.where(box_lane == box, pair_value, 0.0)
        value += table[0:8] + table[8:16] + table[16:24]
    g_sum[0] = value

    def g_copies(stage):
        return [
            remote(
                g_sum.at[stage],
                g_got.at[stage, place],
                g_s.at[stage, place],
                g_r.at[stage, place],
                device,
            )
            for place, device in groups[stage]
        ]

    g_all = [g_copies(stage) for stage in range(3)]

    def g_gather(stage):
        total = g_sum[stage]
        for (place, _), copy in zip(groups[stage], g_all[stage]):
            copy.wait_recv()
            total = total + g_got[stage, place]
        return total

    for copy in g_all[0]:
        copy.start()

    for copy in fars:
        copy.wait_recv()
    far = far_sum[...]
    for k in range(1, NZ):
        far = far + far_got[k]
    far = far * norm_far
    far_re = jnp.broadcast_to(far[:, 0:1], (16, 128))
    far_im = jnp.broadcast_to(far[:, 64:65], (16, 128))

    g_sum[1] = g_gather(0)
    for copy in g_all[1]:
        copy.start()

    inv_copy.wait()
    for way in (0, 1):
        part_copies[way, 1].wait_recv()
    for c in range(blocks):
        re = pl.ds(2 * c, 16, stride=16)
        im = pl.ds(2 * c + 1, 16, stride=16)
        rr, ri = rad[re, :], rad[im, :]
        total = (own_sum[c] + (part_got[0, 0, c] + part_got[1, 0, c])).reshape(32, 128)
        res_re = ((far_re * rr + far_im * ri) - total[0:16]).astype(BF16)
        res_im = ((far_im * rr - far_re * ri) - total[16:32]).astype(BF16)
        lhs[c, 0:16, 0:128] = res_re
        lhs[c, 0:16, 128:256] = res_im
        lhs[c, 16:32, 0:128] = res_im
        lhs[c, 16:32, 128:256] = -res_re
        update = jnp.dot(lhs[c], inv[c], preferred_element_type=F32)
        out[re, :] = adj[re, :] + update[0:16]
        out[im, :] = adj[im, :] + update[16:32]

    g_sum[2] = g_gather(1)
    for copy in g_all[2]:
        copy.start()
    total = jnp.sum(g_gather(2), axis=0, keepdims=True)
    grad[...] = jnp.broadcast_to(total, (8, 128))

    for copy in msgs + fars + g_all[0] + g_all[1] + g_all[2]:
        copy.wait_send()
    for way in (0, 1):
        for step in range(1, 5):
            cur_copies[way, step].wait_send()
            part_copies[way, step].wait_send()

    def terms_gone(place, _):
        for k in range(1, NX):
            term_copy(place, k).wait_send()
        return 0

    lax.fori_loop(0, NZ, terms_gone, 0)


def on_device(
    adjoint,
    currents,
    radiation,
    near_blocks,
    inverse_blocks,
    col_device,
    col_offset,
    box_of_block,
    pair_rate,
):
    angles_here, blocks, unknowns = adjoint.shape[1], adjoint.shape[2], adjoint.shape[4]
    near_count = near_blocks.shape[1]
    pairs = blocks * near_count
    ny, nc = lax.axis_size("angle"), lax.axis_size("pol")
    basis_count = lax.axis_size("basis")
    rows = angles_here * blocks * 2

    me = lax.axis_index("basis")
    target = col_device.reshape(pairs)
    far_x = (target // NZ - me // NZ) % NX
    far_z = (target % NZ - me % NZ) % NZ
    place = sum(jnp.where(far_z == d, i, 0) for i, d in enumerate(ORDER))
    number = lax.iota(jnp.int32, pairs)
    rank = jnp.sum(
        (target[:, None] == target[None, :]) & (number[None, :] < number[:, None]),
        axis=1,
        dtype=jnp.int32,
    )
    slot = (far_x * NZ + place) * CAP + rank
    slots = NX * NZ * CAP
    hot = slot[None, :] == lax.iota(jnp.int32, slots)[:, None]
    pair_tab = jnp.sum(jnp.where(hot, number[None, :], 0), axis=1)
    off = jnp.sum(jnp.where(hot, col_offset.reshape(1, pairs) + 1, 0), axis=1) - 1
    rate = jnp.sum(jnp.where(hot, pair_rate.reshape(1, pairs), 0.0), axis=1)
    box_pairs = jnp.repeat(box_of_block, near_count)
    box = jnp.sum(jnp.where(hot, box_pairs[None, :], 0), axis=1).astype(F32)
    lanes = lax.iota(jnp.int32, 128)[None, :]
    off_tab = jnp.broadcast_to(off.astype(F32)[:, None], (slots, 128)).reshape(NX, NZ * CAP, 128)
    rate_box = jnp.where(lanes < 64, rate[:, None], box[:, None]).reshape(NX, NZ * CAP, 128)

    vmem = pl.BlockSpec(memory_space=pltpu.VMEM)
    anywhere = pl.BlockSpec(memory_space=pl.ANY)
    dma = pltpu.SemaphoreType.DMA
    sizes = (ny, nc, 1.0 / math.sqrt(blocks * basis_count * unknowns))
    out, grad = pl.pallas_call(
        functools.partial(kernel, sizes),
        out_shape=(
            jax.ShapeDtypeStruct((rows, unknowns), F32),
            jax.ShapeDtypeStruct((8, 128), F32),
        ),
        in_specs=[pl.BlockSpec(memory_space=pltpu.SMEM)] + [vmem] * 5 + [anywhere] * 2,
        out_specs=(vmem, vmem),
        scratch_shapes=[
            pltpu.VMEM((pairs, 2 * unknowns, unknowns), BF16),
            pltpu.VMEM((blocks, 2 * unknowns, unknowns), BF16),
            pltpu.VMEM((blocks, 32, 256), BF16),
            pltpu.VMEM((NZ, NX - 1, CAP, 4, 8, 128), F32),
            pltpu.VMEM((NZ, NX, CAP, 4, 8, 128), F32),
            pltpu.VMEM((NZ, blocks, 4, 8, 128), F32),
            pltpu.VMEM((2, 4, blocks, 4, 8, 128), F32),
            pltpu.VMEM((2, 4, blocks, 4, 8, 128), F32),
            pltpu.VMEM((blocks, 4, 8, 128), F32),
            pltpu.VMEM((NX, 64, 128), F32),
            pltpu.VMEM((NX, 64, 128), F32),
            pltpu.VMEM((16, 128), F32),
            pltpu.VMEM((NZ, 16, 128), F32),
            pltpu.VMEM((NX, NZ * CAP, 128), F32),
            pltpu.VMEM((3, 8, 128), F32),
            pltpu.VMEM((3, 8, 8, 128), F32),
            dma((2,)),
            dma((NZ, NX - 1)),
            dma((NZ, NX - 1)),
            dma((2, 4)),
            dma((2, 4)),
            dma((2, 4)),
            dma((2, 4)),
            dma((NX,)),
            dma((NX,)),
            dma((NZ,)),
            dma((NZ,)),
            dma((3, 8)),
            dma((3, 8)),
        ],
        compiler_params=pltpu.CompilerParams(
            collective_id=0, has_side_effects=True, vmem_limit_bytes=40 << 20
        ),
        name="sweep",
    )(
        pair_tab,
        adjoint.reshape(rows, unknowns),
        currents.reshape(rows, unknowns),
        radiation.reshape(rows, unknowns),
        off_tab,
        rate_box,
        near_blocks.reshape(pairs, 2 * unknowns, unknowns),
        inverse_blocks.reshape(blocks, 2 * unknowns, unknowns),
    )
    share = lax.dynamic_slice_in_dim(grad[0], me * BOX_DEV, BOX_DEV)
    angles_all = angles_here * ny
    shape_grad = share * (-1.0 / math.sqrt(4 * unknowns * angles_all * near_count))
    return (out.reshape(adjoint.shape), shape_grad)


def solution(mesh):
    placed = (
        P("pol", "angle", "basis", None, None),
        P("pol", "angle", "basis", None, None),
        P("pol", "angle", "basis", None, None),
        P("basis", None, None, None, None),
        P("basis", None, None, None),
        P("basis", None),
        P("basis", None),
        P("basis"),
        P("basis", None),
    )
    return jax.shard_map(
        on_device,
        mesh=mesh,
        in_specs=placed,
        out_specs=(P("pol", "angle", "basis", None, None), P("basis")),
        check_vma=False,
    )
```

```python
import functools
import math

import jax
import jax.numpy as jnp
from jax import lax
from jax.experimental import pallas as pl
from jax.experimental.pallas import tpu as pltpu
from jax.sharding import PartitionSpec as P

MESH = pl.DeviceIdType.MESH
F32 = jnp.float32
BF16 = jnp.bfloat16

NX, NZ = 4, 8
CAP = 3
BOX_DEV = 4
ORDER = (4, 3, 5, 2, 6, 1, 7, 0)
PLACE = {distance % NZ: place for place, distance in enumerate(ORDER)}


def kernel(
    sizes,
    box_hbm,
    dev_hbm,
    off_hbm,
    rate_hbm,
    adj_hbm,
    cur_hbm,
    rad_hbm,
    near_hbm,
    inv_hbm,
    out,
    grad,
    box_of,
    dev,
    off_of,
    rate_of,
    adj,
    cur,
    rad,
    near,
    inv,
    tab_v,
    pair_tab,
    lhs,
    sent,
    got,
    cur_at,
    part,
    part_got,
    own_sum,
    msg,
    msg_got,
    far_sum,
    far_got,
    lane_dots,
    g_sum,
    g_got,
    local_sem,
    term_s,
    term_r,
    cur_s,
    cur_r,
    part_s,
    part_r,
    msg_s,
    msg_r,
    far_s,
    far_r,
    g_s,
    g_r,
):
    ny, nc, norm_far = sizes
    blocks, near_count = 8, 6
    pairs = blocks * near_count
    half = blocks // 2
    b = lax.axis_index("basis")
    y = lax.axis_index("angle")
    c0 = lax.axis_index("pol")
    x = lax.div(b, NZ)
    z = lax.rem(b, NZ)

    def at(dx=0, dz=0, dy=0, dc=0):
        basis = lax.rem(x + dx, NX) * NZ + lax.rem(z + dz, NZ)
        return (basis, lax.rem(y + dy, ny), lax.rem(c0 + dc, nc))

    def remote(src, dst, send_sem, recv_sem, device):
        return pltpu.make_async_remote_copy(
            src_ref=src,
            dst_ref=dst,
            send_sem=send_sem,
            recv_sem=recv_sem,
            device_id=device,
            device_id_type=MESH,
        )

    loads = [
        pltpu.make_async_copy(src, dst, local_sem.at[i])
        for i, (src, dst) in enumerate(
            [
                (box_hbm, box_of),
                (dev_hbm, dev),
                (off_hbm, off_of),
                (rate_hbm, rate_of),
                (cur_hbm, cur),
                (adj_hbm, adj),
                (rad_hbm, rad),
                (near_hbm, near),
                (inv_hbm, inv),
            ]
        )
    ]
    for copy in loads:
        copy.start()
    box_in, dev_in, off_in, rate_in, cur_in, adj_in, rad_in, near_in, inv_in = loads

    groups = [
        [(dx * nc + dc, at(dx=dx, dc=dc)) for dx in range(NX) for dc in range(nc) if dx or dc],
        [(dz, at(dz=dz)) for dz in range(1, NZ)],
        [(dy, at(dy=dy)) for dy in range(1, ny)],
    ]
    barrier = pltpu.get_barrier_semaphore()
    for group in groups:
        for _, device in group:
            pl.semaphore_signal(barrier, inc=1, device_id=device, device_id_type=MESH)

    for copy in (box_in, dev_in, off_in, rate_in):
        copy.wait()

    def column(values):
        return jnp.concatenate(
            [jnp.broadcast_to(values[:, k : k + 1], (blocks, 128)) for k in range(near_count)]
        )

    sub = lax.broadcasted_iota(jnp.int32, (pairs, 128), 0)
    lane = lax.broadcasted_iota(jnp.int32, (pairs, 128), 1)
    target = column(dev[...].astype(F32))
    target_row = jnp.sum(jnp.where(sub == lane, target, 0.0), axis=0, keepdims=True)
    rank = jnp.sum(
        jnp.where((target == target_row) & (sub < lane), 1.0, 0.0), axis=0, keepdims=True
    )
    device_row = target_row.astype(jnp.int32)
    far_x = (lax.shift_right_logical(device_row, 3) + (NX - x)) & (NX - 1)
    far_z = ((device_row & (NZ - 1)) + (NZ - z)) & (NZ - 1)
    place_row = jnp.zeros((1, 128), jnp.int32)
    for place, distance in enumerate(ORDER):
        place_row = jnp.where(far_z == distance, place, place_row)
    slot_row = ((far_x * NZ + place_row) * CAP).astype(F32) + rank
    slot_row = jnp.where(lane[0:1] < pairs, slot_row, -1.0)
    slot_col = jnp.sum(jnp.where(sub == lane, slot_row, 0.0), axis=1, keepdims=True)
    pair_id = ((sub & (blocks - 1)) * near_count + lax.shift_right_logical(sub, 3)).astype(F32)
    pair_row = jnp.sum(
        jnp.where(slot_col == lane.astype(F32), pair_id, 0.0), axis=0, keepdims=True
    )
    tab_v[...] = jnp.broadcast_to(pair_row, (8, 128)).astype(jnp.int32)
    tab_copy = pltpu.make_async_copy(tab_v, pair_tab, local_sem.at[9])
    tab_copy.start()

    slots = NX * NZ * CAP
    hot = jnp.where(
        slot_row == lax.broadcasted_iota(jnp.int32, (slots, 128), 0).astype(F32), 1.0, 0.0
    )
    rest = jnp.zeros((128 - pairs, 128), F32)
    off_col = jnp.concatenate([column(off_of[...].astype(F32)) + 1.0, rest])
    off_tab = (
        jnp.dot(hot.astype(BF16), off_col.astype(BF16), preferred_element_type=F32) - 1.0
    )
    row = lax.broadcasted_iota(jnp.int32, (blocks, 128), 0)
    box = jnp.zeros((blocks, 128), F32)
    for r in range(blocks):
        box = jnp.where(row == r, box_of[r].astype(F32), box)
    rate_box = jnp.where(
        lane < 64, column(rate_of[...]), jnp.concatenate([box] * near_count)
    )
    rate_box = jnp.dot(
        hot,
        jnp.concatenate([rate_box, rest]),
        precision=lax.Precision.HIGHEST,
        preferred_element_type=F32,
    )

    cur_in.wait()
    for r in range(blocks):
        re = pl.ds(2 * r, 16, stride=16)
        im = pl.ds(2 * r + 1, 16, stride=16)
        cur_at[PLACE[0], r, 0:2] = cur[re, :].reshape(2, 8, 128)
        cur_at[PLACE[0], r, 2:4] = cur[im, :].reshape(2, 8, 128)
    adj_in.wait()
    for r in range(blocks):
        re = pl.ds(2 * r, 16, stride=16)
        im = pl.ds(2 * r + 1, 16, stride=16)
        ar, ai = adj[re, :].astype(BF16), adj[im, :].astype(BF16)
        lhs[r, 0:16, 0:128] = ar
        lhs[r, 0:16, 128:256] = ai
        lhs[r, 16:32, 0:128] = ai
        lhs[r, 16:32, 128:256] = -ar
    rad_in.wait()
    far_re = jnp.zeros((16, 128), F32)
    far_im = jnp.zeros((16, 128), F32)
    for r in range(blocks):
        re = pl.ds(2 * r, 16, stride=16)
        im = pl.ds(2 * r + 1, 16, stride=16)
        rr, ri = rad[re, :], rad[im, :]
        cr, ci = cur[re, :], cur[im, :]
        far_re += rr * cr - ri * ci
        far_im += rr * ci + ri * cr
    far_tile = jnp.where(
        lane[0:16] < 64,
        jnp.sum(far_re, axis=1, keepdims=True),
        jnp.sum(far_im, axis=1, keepdims=True),
    )
    for k in range(NX):
        to = msg if k else msg_got
        rows = slice(k * NZ * CAP, (k + 1) * NZ * CAP)
        to[k, 0:16] = far_tile
        to[k, 16:40] = off_tab[rows]
        to[k, 40:64] = rate_box[rows]
    tab_copy.wait()
    near_in.wait()

    pl.semaphore_wait(barrier, sum(len(group) for group in groups))

    def halves(hops, way):
        return (0, 1) if hops < 4 else (way,)

    def cur_copy(way, step, h):
        sign = 1 if way == 0 else -1
        rows = slice(h * half, (h + 1) * half)
        return remote(
            cur_at.at[PLACE[(-sign * (step - 1)) % NZ], rows],
            cur_at.at[PLACE[(-sign * step) % NZ], rows],
            cur_s.at[way, step - 1, h],
            cur_r.at[way, step - 1, h],
            at(dz=sign % NZ),
        )

    cur_copies = {
        (way, step, h): cur_copy(way, step, h)
        for way in (0, 1)
        for step in range(1, 5)
        for h in halves(step, way)
    }

    def pass_currents(step, h):
        for way in (0, 1):
            cur_copies[way, step - 1, h].wait_recv()
            if h in halves(step, way):
                cur_copies[way, step, h].start()

    for h in (0, 1):
        for way in (0, 1):
            cur_copies[way, 1, h].start()

    def term_copy(place, k):
        return remote(
            sent.at[place, k - 1],
            got.at[place, k],
            term_s.at[place, k - 1],
            term_r.at[place, k - 1],
            at(dx=k),
        )

    def send_terms(place):
        for k in (2, 1, 3, 0):
            for s in range(CAP):
                pair = pair_tab[0, k * NZ * CAP + place * CAP + s]
                pair = jnp.clip(pair, 0, pairs - 1)
                term = jnp.dot(
                    lhs[lax.div(pair, near_count)], near[pair], preferred_element_type=F32
                ).reshape(4, 8, 128)
                if k:
                    sent[place, k - 1, s] = term
                else:
                    got[place, 0, s] = term
            if k:
                term_copy(place, k).start()

    def masks(place, k, s):
        at_row = 16 + place * CAP + s
        off = jnp.broadcast_to(msg_got[k, at_row : at_row + 1, :], (8, 128))
        return [(off == float(c))[None] for c in range(blocks)]

    def combine(place, to):
        for k in range(1, NX):
            term_copy(place, k).wait_recv()
        sums = [jnp.zeros((4, 8, 128), F32) for _ in range(blocks)]
        for k in range(NX):
            for s in range(CAP):
                term = got[place, k, s]
                for c, mask in enumerate(masks(place, k, s)):
                    sums[c] = sums[c] + jnp.where(mask, term, 0.0)
        for c in range(blocks):
            to(c)[...] = sums[c]

    def dots(place):
        for k in range(NX):
            for s in range(CAP):
                chosen = jnp.zeros((4, 8, 128), F32)
                for c, mask in enumerate(masks(place, k, s)):
                    chosen = jnp.where(mask, cur_at[place, c], chosen)
                product = jnp.sum(got[place, k, s] * chosen, axis=0)
                lane_dots[k, place * CAP + s : place * CAP + s + 1, :] = jnp.sum(
                    product, axis=0, keepdims=True
                )

    def part_copy(way, hops, h):
        rows = slice(h * half, (h + 1) * half)
        return remote(
            part.at[way, hops - 1, rows],
            part_got.at[way, hops - 1, rows],
            part_s.at[way, hops - 1, h],
            part_r.at[way, hops - 1, h],
            at(dz=1 if way == 0 else NZ - 1),
        )

    part_copies = {
        (way, hops, h): part_copy(way, hops, h)
        for way in (0, 1)
        for hops in range(1, 5)
        for h in halves(hops, way)
    }

    def combine_ring(hops):
        if hops == 4:
            combine(PLACE[4], lambda c: part.at[c // half, 3, c])
        else:
            combine(PLACE[hops], lambda c: part.at[0, hops - 1, c])
            combine(PLACE[NZ - hops], lambda c: part.at[1, hops - 1, c])

    def pass_sums(hops):
        for h in (0, 1):
            for way in (0, 1):
                if h in halves(hops + 1, way):
                    part_copies[way, hops + 1, h].wait_recv()
                    for c in range(h * half, (h + 1) * half):
                        part[way, hops - 1, c] += part_got[way, hops, c]
                part_copies[way, hops, h].start()

    msgs = [
        remote(msg.at[k], msg_got.at[k], msg_s.at[k], msg_r.at[k], at(dx=k))
        for k in range(1, NX)
    ]
    for copy in msgs:
        copy.start()
    send_terms(0)
    send_terms(1)
    pass_currents(2, 0)
    send_terms(2)
    pass_currents(2, 1)
    send_terms(3)
    for copy in msgs:
        copy.wait_recv()
    combine_ring(4)
    for way in (0, 1):
        part_copies[way, 4, way].start()
    pass_currents(3, 0)
    send_terms(4)
    pass_currents(3, 1)

    far_sum[...] = msg_got[0, 0:16] + msg_got[1, 0:16] + msg_got[2, 0:16] + msg_got[3, 0:16]
    fars = [
        remote(far_sum, far_got.at[k], far_s.at[k], far_r.at[k], at(dz=k)) for k in range(1, NZ)
    ]
    for copy in fars:
        copy.start()

    combine_ring(3)
    pass_sums(3)
    send_terms(5)
    pass_currents(4, 0)
    send_terms(6)
    pass_currents(4, 1)
    send_terms(7)
    combine_ring(2)
    pass_sums(2)
    combine_ring(1)
    for d in (1, 7, 2, 6, 3, 5):
        dots(PLACE[d])
    for way in (0, 1):
        cur_copies[way, 4, way].wait_recv()
    dots(PLACE[4])
    combine(PLACE[0], lambda c: own_sum.at[c])
    dots(PLACE[0])

    value = jnp.zeros((8, 128), F32)
    box_lane = lax.broadcasted_iota(jnp.int32, (NZ * CAP, 128), 1).astype(F32)
    for k in range(NX):
        rate = msg_got[k, 40:64, 0:1]
        box = msg_got[k, 40:64, 64:65]
        pair_value = rate * jnp.sum(lane_dots[k], axis=1, keepdims=True)
        table = jnp.where(box_lane == box, pair_value, 0.0)
        value += table[0:8] + table[8:16] + table[16:24]
    g_sum[0] = value

    g_all = [
        [
            remote(
                g_sum.at[stage],
                g_got.at[stage, place],
                g_s.at[stage, place],
                g_r.at[stage, place],
                device,
            )
            for place, device in groups[stage]
        ]
        for stage in range(3)
    ]

    def g_gather(stage):
        total = g_sum[stage]
        for (place, _), copy in zip(groups[stage], g_all[stage]):
            copy.wait_recv()
            total = total + g_got[stage, place]
        return total

    for copy in g_all[0]:
        copy.start()

    pass_sums(1)

    g_sum[1] = g_gather(0)
    for copy in g_all[1]:
        copy.start()

    for copy in fars:
        copy.wait_recv()
    far = far_sum[...]
    for k in range(1, NZ):
        far = far + far_got[k]
    far = far * norm_far
    far_re = jnp.broadcast_to(far[:, 0:1], (16, 128))
    far_im = jnp.broadcast_to(far[:, 64:65], (16, 128))

    def finish(h):
        for way in (0, 1):
            part_copies[way, 1, h].wait_recv()
        for c in range(h * half, (h + 1) * half):
            re = pl.ds(2 * c, 16, stride=16)
            im = pl.ds(2 * c + 1, 16, stride=16)
            rr, ri = rad[re, :], rad[im, :]
            total = (own_sum[c] + (part_got[0, 0, c] + part_got[1, 0, c])).reshape(32, 128)
            res_re = ((far_re * rr + far_im * ri) - total[0:16]).astype(BF16)
            res_im = ((far_im * rr - far_re * ri) - total[16:32]).astype(BF16)
            lhs[c, 0:16, 0:128] = res_re
            lhs[c, 0:16, 128:256] = res_im
            lhs[c, 16:32, 0:128] = res_im
            lhs[c, 16:32, 128:256] = -res_re
            update = jnp.dot(lhs[c], inv[c], preferred_element_type=F32)
            out[re, :] = adj[re, :] + update[0:16]
            out[im, :] = adj[im, :] + update[16:32]

    inv_in.wait()
    finish(0)
    g_sum[2] = g_gather(1)
    for copy in g_all[2]:
        copy.start()
    finish(1)
    total = jnp.sum(g_gather(2), axis=0, keepdims=True)
    grad[...] = jnp.broadcast_to(total, (8, 128))

    for copy in msgs + fars + g_all[0] + g_all[1] + g_all[2]:
        copy.wait_send()
    for copy in list(cur_copies.values()) + list(part_copies.values()):
        copy.wait_send()
    for place in range(NZ):
        for k in range(1, NX):
            term_copy(place, k).wait_send()


def on_device(
    adjoint,
    currents,
    radiation,
    near_blocks,
    inverse_blocks,
    col_device,
    col_offset,
    box_of_block,
    pair_rate,
):
    angles_here, blocks, unknowns = adjoint.shape[1], adjoint.shape[2], adjoint.shape[4]
    near_count = near_blocks.shape[1]
    pairs = blocks * near_count
    ny, nc = lax.axis_size("angle"), lax.axis_size("pol")
    basis_count = lax.axis_size("basis")
    rows = angles_here * blocks * 2

    vmem = pl.BlockSpec(memory_space=pltpu.VMEM)
    dma = pltpu.SemaphoreType.DMA
    sizes = (ny, nc, 1.0 / math.sqrt(blocks * basis_count * unknowns))
    out, grad = pl.pallas_call(
        functools.partial(kernel, sizes),
        out_shape=(
            jax.ShapeDtypeStruct((rows, unknowns), F32),
            jax.ShapeDtypeStruct((8, 128), F32),
        ),
        in_specs=[pl.BlockSpec(memory_space=pltpu.HBM)] * 9,
        out_specs=(vmem, vmem),
        scratch_shapes=[
            pltpu.SMEM((blocks,), jnp.int32),
            pltpu.VMEM((blocks, near_count), jnp.int32),
            pltpu.VMEM((blocks, near_count), jnp.int32),
            pltpu.VMEM((blocks, near_count), F32),
            pltpu.VMEM((rows, unknowns), F32),
            pltpu.VMEM((rows, unknowns), F32),
            pltpu.VMEM((rows, unknowns), F32),
            pltpu.VMEM((pairs, 2 * unknowns, unknowns), BF16),
            pltpu.VMEM((blocks, 2 * unknowns, unknowns), BF16),
            pltpu.VMEM((8, 128), jnp.int32),
            pltpu.SMEM((8, 128), jnp.int32),
            pltpu.VMEM((blocks, 32, 256), BF16),
            pltpu.VMEM((NZ, NX - 1, CAP, 4, 8, 128), F32),
            pltpu.VMEM((NZ, NX, CAP, 4, 8, 128), F32),
            pltpu.VMEM((NZ, blocks, 4, 8, 128), F32),
            pltpu.VMEM((2, 4, blocks, 4, 8, 128), F32),
            pltpu.VMEM((2, 4, blocks, 4, 8, 128), F32),
            pltpu.VMEM((blocks, 4, 8, 128), F32),
            pltpu.VMEM((NX, 64, 128), F32),
            pltpu.VMEM((NX, 64, 128), F32),
            pltpu.VMEM((16, 128), F32),
            pltpu.VMEM((NZ, 16, 128), F32),
            pltpu.VMEM((NX, NZ * CAP, 128), F32),
            pltpu.VMEM((3, 8, 128), F32),
            pltpu.VMEM((3, 8, 8, 128), F32),
            dma((10,)),
            dma((NZ, NX - 1)),
            dma((NZ, NX - 1)),
            dma((2, 4, 2)),
            dma((2, 4, 2)),
            dma((2, 4, 2)),
            dma((2, 4, 2)),
            dma((NX,)),
            dma((NX,)),
            dma((NZ,)),
            dma((NZ,)),
            dma((3, 8)),
            dma((3, 8)),
        ],
        compiler_params=pltpu.CompilerParams(
            collective_id=0, has_side_effects=True, vmem_limit_bytes=60 << 20
        ),
        name="sweep",
    )(
        box_of_block,
        col_device,
        col_offset,
        pair_rate,
        adjoint.reshape(rows, unknowns),
        currents.reshape(rows, unknowns),
        radiation.reshape(rows, unknowns),
        near_blocks.reshape(pairs, 2 * unknowns, unknowns),
        inverse_blocks.reshape(blocks, 2 * unknowns, unknowns),
    )
    me = lax.axis_index("basis")
    share = lax.dynamic_slice_in_dim(grad[0], me * BOX_DEV, BOX_DEV)
    angles_all = angles_here * ny
    shape_grad = share * (-1.0 / math.sqrt(4 * unknowns * angles_all * near_count))
    return (out.reshape(adjoint.shape), shape_grad)


def solution(mesh):
    placed = (
        P("pol", "angle", "basis", None, None),
        P("pol", "angle", "basis", None, None),
        P("pol", "angle", "basis", None, None),
        P("basis", None, None, None, None),
        P("basis", None, None, None),
        P("basis", None),
        P("basis", None),
        P("basis"),
        P("basis", None),
    )
    return jax.shard_map(
        on_device,
        mesh=mesh,
        in_specs=placed,
        out_specs=(P("pol", "angle", "basis", None, None), P("basis")),
        check_vma=False,
    )
```

```python
import functools
import math

import jax
import jax.numpy as jnp
from jax import lax
from jax.experimental import pallas as pl
from jax.experimental.pallas import tpu as pltpu
from jax.sharding import PartitionSpec as P

MESH = pl.DeviceIdType.MESH
F32 = jnp.float32
BF16 = jnp.bfloat16

NX, NZ = 4, 8
CAP = 3
BOX_DEV = 4
ORDER = (4, 3, 5, 2, 6, 1, 7, 0)
PLACE = {distance % NZ: place for place, distance in enumerate(ORDER)}


def kernel(
    sizes,
    box_hbm,
    dev_hbm,
    off_hbm,
    rate_hbm,
    adj_hbm,
    cur_hbm,
    rad_hbm,
    near_hbm,
    inv_hbm,
    out,
    grad,
    box_of,
    dev,
    off_of,
    rate_of,
    adj,
    cur,
    rad,
    near,
    inv,
    tab_v,
    pair_tab,
    lhs,
    sent,
    got,
    cur_at,
    part,
    part_got,
    own_sum,
    msg,
    msg_got,
    far_sum,
    far_got,
    lane_dots,
    g_sum,
    g_got,
    local_sem,
    term_s,
    term_r,
    cur_s,
    cur_r,
    part_s,
    part_r,
    msg_s,
    msg_r,
    far_s,
    far_r,
    g_s,
    g_r,
):
    ny, nc, norm_far, grad_norm = sizes
    blocks, near_count = 8, 6
    pairs = blocks * near_count
    half = blocks // 2
    b = lax.axis_index("basis")
    y = lax.axis_index("angle")
    c0 = lax.axis_index("pol")
    x = lax.div(b, NZ)
    z = lax.rem(b, NZ)

    def at(dx=0, dz=0, dy=0, dc=0):
        basis = lax.rem(x + dx, NX) * NZ + lax.rem(z + dz, NZ)
        return (basis, lax.rem(y + dy, ny), lax.rem(c0 + dc, nc))

    def remote(src, dst, send_sem, recv_sem, device):
        return pltpu.make_async_remote_copy(
            src_ref=src,
            dst_ref=dst,
            send_sem=send_sem,
            recv_sem=recv_sem,
            device_id=device,
            device_id_type=MESH,
        )

    loads = [
        pltpu.make_async_copy(src, dst, local_sem.at[i])
        for i, (src, dst) in enumerate(
            [
                (box_hbm, box_of),
                (dev_hbm, dev),
                (off_hbm, off_of),
                (rate_hbm, rate_of),
                (cur_hbm, cur),
                (adj_hbm, adj),
                (rad_hbm, rad),
                (near_hbm, near),
                (inv_hbm, inv),
            ]
        )
    ]
    for copy in loads:
        copy.start()
    box_in, dev_in, off_in, rate_in, cur_in, adj_in, rad_in, near_in, inv_in = loads

    groups = [
        [(dx * nc + dc, at(dx=dx, dc=dc)) for dx in range(NX) for dc in range(nc) if dx or dc],
        [(dz, at(dz=dz)) for dz in range(1, NZ)],
        [(dy, at(dy=dy)) for dy in range(1, ny)],
    ]
    barrier = pltpu.get_barrier_semaphore()
    for group in groups:
        for _, device in group:
            pl.semaphore_signal(barrier, inc=1, device_id=device, device_id_type=MESH)

    for copy in (box_in, dev_in, off_in, rate_in):
        copy.wait()

    def column(values):
        return jnp.concatenate(
            [jnp.broadcast_to(values[:, k : k + 1], (blocks, 128)) for k in range(near_count)]
        )

    sub = lax.broadcasted_iota(jnp.int32, (pairs, 128), 0)
    lane = lax.broadcasted_iota(jnp.int32, (pairs, 128), 1)
    target = column(dev[...].astype(F32))
    target_row = jnp.sum(jnp.where(sub == lane, target, 0.0), axis=0, keepdims=True)
    rank = jnp.sum(
        jnp.where((target == target_row) & (sub < lane), 1.0, 0.0), axis=0, keepdims=True
    )
    device_row = target_row.astype(jnp.int32)
    far_x = (lax.shift_right_logical(device_row, 3) + (NX - x)) & (NX - 1)
    far_z = ((device_row & (NZ - 1)) + (NZ - z)) & (NZ - 1)
    place_row = jnp.zeros((1, 128), jnp.int32)
    for place, distance in enumerate(ORDER):
        place_row = jnp.where(far_z == distance, place, place_row)
    slot_row = ((far_x * NZ + place_row) * CAP).astype(F32) + rank
    slot_row = jnp.where(lane[0:1] < pairs, slot_row, -1.0)
    slot_col = jnp.sum(jnp.where(sub == lane, slot_row, 0.0), axis=1, keepdims=True)
    pair_id = ((sub & (blocks - 1)) * near_count + lax.shift_right_logical(sub, 3)).astype(F32)
    pair_row = jnp.sum(
        jnp.where(slot_col == lane.astype(F32), pair_id, 0.0), axis=0, keepdims=True
    )
    tab_v[...] = jnp.broadcast_to(pair_row, (8, 128)).astype(jnp.int32)
    tab_copy = pltpu.make_async_copy(tab_v, pair_tab, local_sem.at[9])
    tab_copy.start()

    slots = NX * NZ * CAP
    hot = jnp.where(
        slot_row == lax.broadcasted_iota(jnp.int32, (slots, 128), 0).astype(F32), 1.0, 0.0
    )
    rest = jnp.zeros((128 - pairs, 128), F32)
    off_col = jnp.concatenate([column(off_of[...].astype(F32)) + 1.0, rest])
    off_tab = (
        jnp.dot(hot.astype(BF16), off_col.astype(BF16), preferred_element_type=F32) - 1.0
    )
    row = lax.broadcasted_iota(jnp.int32, (blocks, 128), 0)
    box = jnp.zeros((blocks, 128), F32)
    for r in range(blocks):
        box = jnp.where(row == r, box_of[r].astype(F32), box)
    rate_box = jnp.where(
        lane < 64, column(rate_of[...]), jnp.concatenate([box] * near_count)
    )
    rate_box = jnp.dot(
        hot,
        jnp.concatenate([rate_box, rest]),
        precision=lax.Precision.HIGHEST,
        preferred_element_type=F32,
    )

    cur_in.wait()
    for r in range(blocks):
        re = pl.ds(2 * r, 16, stride=16)
        im = pl.ds(2 * r + 1, 16, stride=16)
        cur_at[PLACE[0], r, 0:2] = cur[re, :].reshape(2, 8, 128)
        cur_at[PLACE[0], r, 2:4] = cur[im, :].reshape(2, 8, 128)
    adj_in.wait()
    for r in range(blocks):
        re = pl.ds(2 * r, 16, stride=16)
        im = pl.ds(2 * r + 1, 16, stride=16)
        ar, ai = adj[re, :].astype(BF16), adj[im, :].astype(BF16)
        lhs[r, 0:16, 0:128] = ar
        lhs[r, 0:16, 128:256] = ai
        lhs[r, 16:32, 0:128] = ai
        lhs[r, 16:32, 128:256] = -ar
    rad_in.wait()
    far_re = jnp.zeros((16, 128), F32)
    far_im = jnp.zeros((16, 128), F32)
    for r in range(blocks):
        re = pl.ds(2 * r, 16, stride=16)
        im = pl.ds(2 * r + 1, 16, stride=16)
        rr, ri = rad[re, :], rad[im, :]
        cr, ci = cur[re, :], cur[im, :]
        far_re += rr * cr - ri * ci
        far_im += rr * ci + ri * cr
    far_tile = jnp.where(
        lane[0:16] < 64,
        jnp.sum(far_re, axis=1, keepdims=True),
        jnp.sum(far_im, axis=1, keepdims=True),
    )
    for k in range(NX):
        to = msg if k else msg_got
        rows = slice(k * NZ * CAP, (k + 1) * NZ * CAP)
        to[k, 0:16] = far_tile
        to[k, 16:40] = off_tab[rows]
        to[k, 40:64] = rate_box[rows]
    tab_copy.wait()
    near_in.wait()

    pl.semaphore_wait(barrier, sum(len(group) for group in groups))

    def halves(hops, way):
        return (0, 1) if hops < 4 else (way,)

    def cur_copy(way, step, h):
        sign = 1 if way == 0 else -1
        rows = slice(h * half, (h + 1) * half)
        return remote(
            cur_at.at[PLACE[(-sign * (step - 1)) % NZ], rows],
            cur_at.at[PLACE[(-sign * step) % NZ], rows],
            cur_s.at[way, step - 1, h],
            cur_r.at[way, step - 1, h],
            at(dz=sign % NZ),
        )

    cur_copies = {
        (way, step, h): cur_copy(way, step, h)
        for way in (0, 1)
        for step in range(1, 5)
        for h in halves(step, way)
    }

    def pass_currents(step, h):
        for way in (0, 1):
            cur_copies[way, step - 1, h].wait_recv()
            if h in halves(step, way):
                cur_copies[way, step, h].start()

    for h in (0, 1):
        for way in (0, 1):
            cur_copies[way, 1, h].start()

    def term_copy(place, k):
        return remote(
            sent.at[place, k - 1],
            got.at[place, k],
            term_s.at[place, k - 1],
            term_r.at[place, k - 1],
            at(dx=k),
        )

    def send_terms(place):
        for k in (2, 1, 3, 0):
            for s in range(CAP):
                pair = pair_tab[0, k * NZ * CAP + place * CAP + s]
                pair = jnp.clip(pair, 0, pairs - 1)
                term = jnp.dot(
                    lhs[lax.div(pair, near_count)], near[pair], preferred_element_type=F32
                ).reshape(4, 8, 128)
                if k:
                    sent[place, k - 1, s] = term
                else:
                    got[place, 0, s] = term
            if k:
                term_copy(place, k).start()

    def terms_gone(place):
        for k in range(1, NX):
            term_copy(place, k).wait_send()

    def masks(place, k, s):
        at_row = 16 + place * CAP + s
        off = jnp.broadcast_to(msg_got[k, at_row : at_row + 1, :], (8, 128))
        return [(off == float(c))[None] for c in range(blocks)]

    def combine(place, to):
        for k in range(1, NX):
            term_copy(place, k).wait_recv()
        sums = [jnp.zeros((4, 8, 128), F32) for _ in range(blocks)]
        for k in range(NX):
            for s in range(CAP):
                term = got[place, k, s]
                for c, mask in enumerate(masks(place, k, s)):
                    sums[c] = sums[c] + jnp.where(mask, term, 0.0)
        for c in range(blocks):
            to(c)[...] = sums[c]

    def dots(place):
        for k in range(NX):
            for s in range(CAP):
                chosen = jnp.zeros((4, 8, 128), F32)
                for c, mask in enumerate(masks(place, k, s)):
                    chosen = jnp.where(mask, cur_at[place, c], chosen)
                product = jnp.sum(got[place, k, s] * chosen, axis=0)
                lane_dots[k, place * CAP + s : place * CAP + s + 1, :] = jnp.sum(
                    product, axis=0, keepdims=True
                )

    def part_copy(way, hops, h):
        rows = slice(h * half, (h + 1) * half)
        return remote(
            part.at[way, hops - 1, rows],
            part_got.at[way, hops - 1, rows],
            part_s.at[way, hops - 1, h],
            part_r.at[way, hops - 1, h],
            at(dz=1 if way == 0 else NZ - 1),
        )

    part_copies = {
        (way, hops, h): part_copy(way, hops, h)
        for way in (0, 1)
        for hops in range(1, 5)
        for h in halves(hops, way)
    }

    def combine_ring(hops):
        if hops == 4:
            combine(PLACE[4], lambda c: part.at[c // half, 3, c])
        else:
            combine(PLACE[hops], lambda c: part.at[0, hops - 1, c])
            combine(PLACE[NZ - hops], lambda c: part.at[1, hops - 1, c])

    def pass_sums(hops):
        for h in (0, 1):
            for way in (0, 1):
                if h in halves(hops + 1, way):
                    part_copies[way, hops + 1, h].wait_recv()
                    for c in range(h * half, (h + 1) * half):
                        part[way, hops - 1, c] += part_got[way, hops, c]
                part_copies[way, hops, h].start()

    msgs = [
        remote(msg.at[k], msg_got.at[k], msg_s.at[k], msg_r.at[k], at(dx=k))
        for k in range(1, NX)
    ]
    for copy in msgs:
        copy.start()
    send_terms(0)
    send_terms(1)
    pass_currents(2, 0)
    send_terms(2)
    pass_currents(2, 1)
    send_terms(3)
    for copy in msgs:
        copy.wait_recv()
    combine_ring(4)
    for way in (0, 1):
        part_copies[way, 4, way].start()
    pass_currents(3, 0)
    send_terms(4)
    pass_currents(3, 1)
    far_sum[...] = msg_got[0, 0:16] + msg_got[1, 0:16] + msg_got[2, 0:16] + msg_got[3, 0:16]
    fars = [
        remote(far_sum, far_got.at[k], far_s.at[k], far_r.at[k], at(dz=k)) for k in range(1, NZ)
    ]
    for copy in fars:
        copy.start()
    combine_ring(3)
    pass_sums(3)
    send_terms(5)
    pass_currents(4, 0)
    send_terms(6)
    pass_currents(4, 1)
    send_terms(7)
    combine_ring(2)
    pass_sums(2)
    combine_ring(1)
    dots(PLACE[1])
    dots(PLACE[7])
    dots(PLACE[2])
    dots(PLACE[6])
    dots(PLACE[3])
    dots(PLACE[5])
    for way in (0, 1):
        cur_copies[way, 4, way].wait_recv()
    dots(PLACE[4])
    combine(PLACE[0], lambda c: own_sum.at[c])
    dots(PLACE[0])

    value = jnp.zeros((8, 128), F32)
    box_lane = lax.broadcasted_iota(jnp.int32, (NZ * CAP, 128), 1).astype(F32)
    for k in range(NX):
        rate = msg_got[k, 40:64, 0:1]
        box = msg_got[k, 40:64, 64:65]
        pair_value = rate * jnp.sum(lane_dots[k], axis=1, keepdims=True)
        table = jnp.where(box_lane == box, pair_value, 0.0)
        value += table[0:8] + table[8:16] + table[16:24]
    g_sum[0] = value

    g_all = [
        [
            remote(
                g_sum.at[stage],
                g_got.at[stage, place],
                g_s.at[stage, place],
                g_r.at[stage, place],
                device,
            )
            for place, device in groups[stage]
        ]
        for stage in range(3)
    ]

    def g_gather(stage):
        total = g_sum[stage]
        for (place, _), copy in zip(groups[stage], g_all[stage]):
            copy.wait_recv()
            total = total + g_got[stage, place]
        return total

    for copy in g_all[0]:
        copy.start()
    pass_sums(1)
    g_sum[1] = g_gather(0)
    for copy in g_all[1]:
        copy.start()

    for copy in fars:
        copy.wait_recv()
    far = far_sum[...]
    for k in range(1, NZ):
        far = far + far_got[k]
    far = far * norm_far
    far_re = jnp.broadcast_to(far[:, 0:1], (16, 128))
    far_im = jnp.broadcast_to(far[:, 64:65], (16, 128))

    def finish(h):
        for way in (0, 1):
            part_copies[way, 1, h].wait_recv()
        for c in range(h * half, (h + 1) * half):
            re = pl.ds(2 * c, 16, stride=16)
            im = pl.ds(2 * c + 1, 16, stride=16)
            rr, ri = rad[re, :], rad[im, :]
            total = (own_sum[c] + (part_got[0, 0, c] + part_got[1, 0, c])).reshape(32, 128)
            res_re = ((far_re * rr + far_im * ri) - total[0:16]).astype(BF16)
            res_im = ((far_im * rr - far_re * ri) - total[16:32]).astype(BF16)
            lhs[c, 0:16, 0:128] = res_re
            lhs[c, 0:16, 128:256] = res_im
            lhs[c, 16:32, 0:128] = res_im
            lhs[c, 16:32, 128:256] = -res_re
            update = jnp.dot(lhs[c], inv[c], preferred_element_type=F32)
            out[re, :] = adj[re, :] + update[0:16]
            out[im, :] = adj[im, :] + update[16:32]

    inv_in.wait()
    finish(0)
    g_sum[2] = g_gather(1)
    for copy in g_all[2]:
        copy.start()
    finish(1)
    total = jnp.sum(g_gather(2), axis=0, keepdims=True)
    for i in range(BOX_DEV):
        mine = lane[0:1] == b * BOX_DEV + i
        grad[:, i : i + 1] = jnp.sum(jnp.where(mine, total, 0.0), axis=1, keepdims=True) * grad_norm

    for copy in msgs + fars + g_all[0] + g_all[1] + g_all[2]:
        copy.wait_send()
    for copy in list(cur_copies.values()) + list(part_copies.values()):
        copy.wait_send()
    for place in (0, 1, 2, 3, 4, 5, 6, 7):
        terms_gone(place)


def on_device(
    adjoint,
    currents,
    radiation,
    near_blocks,
    inverse_blocks,
    col_device,
    col_offset,
    box_of_block,
    pair_rate,
):
    angles_here, blocks, unknowns = adjoint.shape[1], adjoint.shape[2], adjoint.shape[4]
    near_count = near_blocks.shape[1]
    pairs = blocks * near_count
    ny, nc = lax.axis_size("angle"), lax.axis_size("pol")
    basis_count = lax.axis_size("basis")
    rows = angles_here * blocks * 2

    vmem = pl.BlockSpec(memory_space=pltpu.VMEM)
    dma = pltpu.SemaphoreType.DMA
    sizes = (
        ny,
        nc,
        1.0 / math.sqrt(blocks * basis_count * unknowns),
        -1.0 / math.sqrt(4 * unknowns * angles_here * ny * near_count),
    )
    out, grad = pl.pallas_call(
        functools.partial(kernel, sizes),
        out_shape=(
            jax.ShapeDtypeStruct((rows, unknowns), F32),
            jax.ShapeDtypeStruct((1, BOX_DEV), F32),
        ),
        in_specs=[pl.BlockSpec(memory_space=pltpu.HBM)] * 9,
        out_specs=(vmem, vmem),
        scratch_shapes=[
            pltpu.SMEM((blocks,), jnp.int32),
            pltpu.VMEM((blocks, near_count), jnp.int32),
            pltpu.VMEM((blocks, near_count), jnp.int32),
            pltpu.VMEM((blocks, near_count), F32),
            pltpu.VMEM((rows, unknowns), F32),
            pltpu.VMEM((rows, unknowns), F32),
            pltpu.VMEM((rows, unknowns), F32),
            pltpu.VMEM((pairs, 2 * unknowns, unknowns), BF16),
            pltpu.VMEM((blocks, 2 * unknowns, unknowns), BF16),
            pltpu.VMEM((8, 128), jnp.int32),
            pltpu.SMEM((8, 128), jnp.int32),
            pltpu.VMEM((blocks, 32, 256), BF16),
            pltpu.VMEM((NZ, NX - 1, CAP, 4, 8, 128), F32),
            pltpu.VMEM((NZ, NX, CAP, 4, 8, 128), F32),
            pltpu.VMEM((NZ, blocks, 4, 8, 128), F32),
            pltpu.VMEM((2, 4, blocks, 4, 8, 128), F32),
            pltpu.VMEM((2, 4, blocks, 4, 8, 128), F32),
            pltpu.VMEM((blocks, 4, 8, 128), F32),
            pltpu.VMEM((NX, 64, 128), F32),
            pltpu.VMEM((NX, 64, 128), F32),
            pltpu.VMEM((16, 128), F32),
            pltpu.VMEM((NZ, 16, 128), F32),
            pltpu.VMEM((NX, NZ * CAP, 128), F32),
            pltpu.VMEM((3, 8, 128), F32),
            pltpu.VMEM((3, 8, 8, 128), F32),
            dma((10,)),
            dma((NZ, NX - 1)),
            dma((NZ, NX - 1)),
            dma((2, 4, 2)),
            dma((2, 4, 2)),
            dma((2, 4, 2)),
            dma((2, 4, 2)),
            dma((NX,)),
            dma((NX,)),
            dma((NZ,)),
            dma((NZ,)),
            dma((3, 8)),
            dma((3, 8)),
        ],
        compiler_params=pltpu.CompilerParams(
            collective_id=0, has_side_effects=True, vmem_limit_bytes=40 << 20
        ),
        name="sweep",
    )(*[pltpu.with_memory_space_constraint(a, pltpu.HBM) for a in (
        box_of_block,
        col_device,
        col_offset,
        pair_rate,
        adjoint.reshape(rows, unknowns),
        currents.reshape(rows, unknowns),
        radiation.reshape(rows, unknowns),
        near_blocks.reshape(pairs, 2 * unknowns, unknowns),
        inverse_blocks.reshape(blocks, 2 * unknowns, unknowns),
    )])
    return (out.reshape(adjoint.shape), grad.reshape(BOX_DEV))


def solution(mesh):
    placed = (
        P("pol", "angle", "basis", None, None),
        P("pol", "angle", "basis", None, None),
        P("pol", "angle", "basis", None, None),
        P("basis", None, None, None, None),
        P("basis", None, None, None),
        P("basis", None),
        P("basis", None),
        P("basis"),
        P("basis", None),
    )
    return jax.shard_map(
        on_device,
        mesh=mesh,
        in_specs=placed,
        out_specs=(P("pol", "angle", "basis", None, None), P("basis")),
        check_vma=False,
    )
```

```python
import functools
import math

import jax
import jax.numpy as jnp
from jax import lax
from jax.experimental import pallas as pl
from jax.experimental.pallas import tpu as pltpu
from jax.sharding import PartitionSpec as P

MESH = pl.DeviceIdType.MESH
F32 = jnp.float32
BF16 = jnp.bfloat16

NX, NZ = 4, 8
CAP = 3
BOX_DEV = 4
ORDER = (4, 3, 5, 2, 6, 1, 7, 0)
PLACE = {distance % NZ: place for place, distance in enumerate(ORDER)}


def kernel(
    sizes,
    box_hbm,
    dev_hbm,
    off_hbm,
    rate_hbm,
    adj_hbm,
    cur_hbm,
    rad_hbm,
    near_hbm,
    inv_hbm,
    out,
    grad,
    box_of,
    dev,
    off_of,
    rate_of,
    adj,
    cur,
    rad,
    near,
    inv,
    tab_v,
    pair_tab,
    lhs,
    sent,
    got,
    cur_at,
    part,
    part_got,
    own_sum,
    msg,
    msg_got,
    far_sum,
    far_got,
    lane_dots,
    g_sum,
    g_got,
    local_sem,
    term_s,
    term_r,
    cur_s,
    cur_r,
    part_s,
    part_r,
    msg_s,
    msg_r,
    far_s,
    far_r,
    g_s,
    g_r,
):
    ny, nc, norm_far, grad_norm = sizes
    blocks, near_count = 8, 6
    pairs = blocks * near_count
    half = blocks // 2
    b = lax.axis_index("basis")
    y = lax.axis_index("angle")
    c0 = lax.axis_index("pol")
    x = lax.div(b, NZ)
    z = lax.rem(b, NZ)

    def at(dx=0, dz=0, dy=0, dc=0):
        basis = lax.rem(x + dx, NX) * NZ + lax.rem(z + dz, NZ)
        return (basis, lax.rem(y + dy, ny), lax.rem(c0 + dc, nc))

    def remote(src, dst, send_sem, recv_sem, device):
        return pltpu.make_async_remote_copy(
            src_ref=src,
            dst_ref=dst,
            send_sem=send_sem,
            recv_sem=recv_sem,
            device_id=device,
            device_id_type=MESH,
        )

    loads = [
        pltpu.make_async_copy(src, dst, local_sem.at[i])
        for i, (src, dst) in enumerate(
            [
                (box_hbm, box_of),
                (dev_hbm, dev),
                (off_hbm, off_of),
                (rate_hbm, rate_of),
                (cur_hbm, cur),
                (adj_hbm, adj),
                (rad_hbm, rad),
                (near_hbm, near),
                (inv_hbm, inv),
            ]
        )
    ]
    for copy in loads:
        copy.start()
    box_in, dev_in, off_in, rate_in, cur_in, adj_in, rad_in, near_in, inv_in = loads

    groups = [
        [(dx * nc + dc, at(dx=dx, dc=dc)) for dx in range(NX) for dc in range(nc) if dx or dc],
        [(dz, at(dz=dz)) for dz in range(1, NZ)],
        [(dy, at(dy=dy)) for dy in range(1, ny)],
    ]
    barrier = pltpu.get_barrier_semaphore()
    for group in groups:
        for _, device in group:
            pl.semaphore_signal(barrier, inc=1, device_id=device, device_id_type=MESH)

    for copy in (box_in, dev_in, off_in, rate_in):
        copy.wait()

    def column(values):
        return jnp.concatenate(
            [jnp.broadcast_to(values[:, k : k + 1], (blocks, 128)) for k in range(near_count)]
        )

    sub = lax.broadcasted_iota(jnp.int32, (pairs, 128), 0)
    lane = lax.broadcasted_iota(jnp.int32, (pairs, 128), 1)
    target = column(dev[...].astype(F32))
    target_row = jnp.sum(jnp.where(sub == lane, target, 0.0), axis=0, keepdims=True)
    rank = jnp.sum(
        jnp.where((target == target_row) & (sub < lane), 1.0, 0.0), axis=0, keepdims=True
    )
    device_row = target_row.astype(jnp.int32)
    far_x = (lax.shift_right_logical(device_row, 3) + (NX - x)) & (NX - 1)
    far_z = ((device_row & (NZ - 1)) + (NZ - z)) & (NZ - 1)
    place_row = jnp.zeros((1, 128), jnp.int32)
    for place, distance in enumerate(ORDER):
        place_row = jnp.where(far_z == distance, place, place_row)
    slot_row = ((far_x * NZ + place_row) * CAP).astype(F32) + rank
    slot_row = jnp.where(lane[0:1] < pairs, slot_row, -1.0)
    slot_col = jnp.sum(jnp.where(sub == lane, slot_row, 0.0), axis=1, keepdims=True)
    pair_id = ((sub & (blocks - 1)) * near_count + lax.shift_right_logical(sub, 3)).astype(F32)
    pair_row = jnp.sum(
        jnp.where(slot_col == lane.astype(F32), pair_id, 0.0), axis=0, keepdims=True
    )
    tab_v[...] = jnp.broadcast_to(pair_row, (8, 128)).astype(jnp.int32)
    tab_copy = pltpu.make_async_copy(tab_v, pair_tab, local_sem.at[9])
    tab_copy.start()

    slots = NX * NZ * CAP
    hot = jnp.where(
        slot_row == lax.broadcasted_iota(jnp.int32, (slots, 128), 0).astype(F32), 1.0, 0.0
    )
    rest = jnp.zeros((128 - pairs, 128), F32)
    off_col = jnp.concatenate([column(off_of[...].astype(F32)) + 1.0, rest])
    off_tab = (
        jnp.dot(hot.astype(BF16), off_col.astype(BF16), preferred_element_type=F32) - 1.0
    )
    row = lax.broadcasted_iota(jnp.int32, (blocks, 128), 0)
    box = jnp.zeros((blocks, 128), F32)
    for r in range(blocks):
        box = jnp.where(row == r, box_of[r].astype(F32), box)
    rate_box = jnp.where(
        lane < 64, column(rate_of[...]), jnp.concatenate([box] * near_count)
    )
    rate_box = jnp.dot(
        hot,
        jnp.concatenate([rate_box, rest]),
        precision=lax.Precision.HIGHEST,
        preferred_element_type=F32,
    )

    cur_in.wait()
    for r in range(blocks):
        re = pl.ds(2 * r, 16, stride=16)
        im = pl.ds(2 * r + 1, 16, stride=16)
        cur_at[PLACE[0], r, 0:2] = cur[re, :].reshape(2, 8, 128)
        cur_at[PLACE[0], r, 2:4] = cur[im, :].reshape(2, 8, 128)
    adj_in.wait()
    for r in range(blocks):
        re = pl.ds(2 * r, 16, stride=16)
        im = pl.ds(2 * r + 1, 16, stride=16)
        ar, ai = adj[re, :].astype(BF16), adj[im, :].astype(BF16)
        lhs[r, 0:16, 0:128] = ar
        lhs[r, 0:16, 128:256] = ai
        lhs[r, 16:32, 0:128] = ai
        lhs[r, 16:32, 128:256] = -ar
    rad_in.wait()
    far_re = jnp.zeros((16, 128), F32)
    far_im = jnp.zeros((16, 128), F32)
    for r in range(blocks):
        re = pl.ds(2 * r, 16, stride=16)
        im = pl.ds(2 * r + 1, 16, stride=16)
        rr, ri = rad[re, :], rad[im, :]
        cr, ci = cur[re, :], cur[im, :]
        far_re += rr * cr - ri * ci
        far_im += rr * ci + ri * cr
    far_tile = jnp.where(
        lane[0:16] < 64,
        jnp.sum(far_re, axis=1, keepdims=True),
        jnp.sum(far_im, axis=1, keepdims=True),
    )
    for k in range(NX):
        to = msg if k else msg_got
        rows = slice(k * NZ * CAP, (k + 1) * NZ * CAP)
        to[k, 0:16] = far_tile
        to[k, 16:40] = off_tab[rows]
        to[k, 40:64] = rate_box[rows]
    tab_copy.wait()
    near_in.wait()

    pl.semaphore_wait(barrier, sum(len(group) for group in groups))

    def halves(hops, way):
        return (0, 1) if hops < 4 else (way,)

    def cur_copy(way, step, h):
        sign = 1 if way == 0 else -1
        rows = slice(h * half, (h + 1) * half)
        return remote(
            cur_at.at[PLACE[(-sign * (step - 1)) % NZ], rows],
            cur_at.at[PLACE[(-sign * step) % NZ], rows],
            cur_s.at[way, step - 1, h],
            cur_r.at[way, step - 1, h],
            at(dz=sign % NZ),
        )

    cur_copies = {
        (way, step, h): cur_copy(way, step, h)
        for way in (0, 1)
        for step in range(1, 5)
        for h in halves(step, way)
    }

    def pass_currents(step, h):
        for way in (0, 1):
            cur_copies[way, step - 1, h].wait_recv()
            if h in halves(step, way):
                cur_copies[way, step, h].start()

    for h in (0, 1):
        for way in (0, 1):
            cur_copies[way, 1, h].start()

    def term_copy(place, k):
        return remote(
            sent.at[place, k - 1],
            got.at[place, k],
            term_s.at[place, k - 1],
            term_r.at[place, k - 1],
            at(dx=k),
        )

    def send_terms(place):
        for k in (2, 1, 3, 0):
            for s in range(CAP):
                pair = pair_tab[0, k * NZ * CAP + place * CAP + s]
                pair = jnp.clip(pair, 0, pairs - 1)
                term = jnp.dot(
                    lhs[lax.div(pair, near_count)], near[pair], preferred_element_type=F32
                ).reshape(4, 8, 128)
                if k:
                    sent[place, k - 1, s] = term
                else:
                    got[place, 0, s] = term
            if k:
                term_copy(place, k).start()

    def terms_gone(place):
        for k in range(1, NX):
            term_copy(place, k).wait_send()

    def masks(place, k, s):
        at_row = 16 + place * CAP + s
        off = jnp.broadcast_to(msg_got[k, at_row : at_row + 1, :], (8, 128))
        return [(off == float(c))[None] for c in range(blocks)]

    def combine(place, to):
        for k in range(1, NX):
            term_copy(place, k).wait_recv()
        sums = [jnp.zeros((4, 8, 128), F32) for _ in range(blocks)]
        for k in range(NX):
            for s in range(CAP):
                term = got[place, k, s]
                for c, mask in enumerate(masks(place, k, s)):
                    sums[c] = sums[c] + jnp.where(mask, term, 0.0)
        for c in range(blocks):
            to(c)[...] = sums[c]

    def dots(place):
        for k in range(NX):
            for s in range(CAP):
                chosen = jnp.zeros((4, 8, 128), F32)
                for c, mask in enumerate(masks(place, k, s)):
                    chosen = jnp.where(mask, cur_at[place, c], chosen)
                product = jnp.sum(got[place, k, s] * chosen, axis=0)
                lane_dots[k, place * CAP + s : place * CAP + s + 1, :] = jnp.sum(
                    product, axis=0, keepdims=True
                )

    def part_copy(way, hops, h):
        rows = slice(h * half, (h + 1) * half)
        return remote(
            part.at[way, hops - 1, rows],
            part_got.at[way, hops - 1, rows],
            part_s.at[way, hops - 1, h],
            part_r.at[way, hops - 1, h],
            at(dz=1 if way == 0 else NZ - 1),
        )

    part_copies = {
        (way, hops, h): part_copy(way, hops, h)
        for way in (0, 1)
        for hops in range(1, 5)
        for h in halves(hops, way)
    }

    def combine_ring(hops):
        if hops == 4:
            combine(PLACE[4], lambda c: part.at[c // half, 3, c])
        else:
            combine(PLACE[hops], lambda c: part.at[0, hops - 1, c])
            combine(PLACE[NZ - hops], lambda c: part.at[1, hops - 1, c])

    def pass_sums(hops):
        for h in (0, 1):
            for way in (0, 1):
                if h in halves(hops + 1, way):
                    part_copies[way, hops + 1, h].wait_recv()
                    for c in range(h * half, (h + 1) * half):
                        part[way, hops - 1, c] += part_got[way, hops, c]
                part_copies[way, hops, h].start()

    msgs = [
        remote(msg.at[k], msg_got.at[k], msg_s.at[k], msg_r.at[k], at(dx=k))
        for k in range(1, NX)
    ]
    for copy in msgs:
        copy.start()
    send_terms(0)
    send_terms(1)
    pass_currents(2, 0)
    send_terms(2)
    pass_currents(2, 1)
    send_terms(3)
    for copy in msgs:
        copy.wait_recv()
    combine_ring(4)
    for way in (0, 1):
        part_copies[way, 4, way].start()
    pass_currents(3, 0)
    send_terms(4)
    pass_currents(3, 1)
    far_sum[...] = msg_got[0, 0:16] + msg_got[1, 0:16] + msg_got[2, 0:16] + msg_got[3, 0:16]
    fars = [
        remote(far_sum, far_got.at[k], far_s.at[k], far_r.at[k], at(dz=k)) for k in range(1, NZ)
    ]
    for copy in fars:
        copy.start()
    combine_ring(3)
    pass_sums(3)
    send_terms(5)
    pass_currents(4, 0)
    send_terms(6)
    pass_currents(4, 1)
    send_terms(7)
    combine_ring(2)
    pass_sums(2)
    combine_ring(1)
    dots(PLACE[1])
    dots(PLACE[7])
    dots(PLACE[2])
    dots(PLACE[6])
    dots(PLACE[3])
    dots(PLACE[5])
    for way in (0, 1):
        cur_copies[way, 4, way].wait_recv()
    dots(PLACE[4])
    combine(PLACE[0], lambda c: own_sum.at[c])
    dots(PLACE[0])

    value = jnp.zeros((8, 128), F32)
    box_lane = lax.broadcasted_iota(jnp.int32, (NZ * CAP, 128), 1).astype(F32)
    for k in range(NX):
        rate = msg_got[k, 40:64, 0:1]
        box = msg_got[k, 40:64, 64:65]
        pair_value = rate * jnp.sum(lane_dots[k], axis=1, keepdims=True)
        table = jnp.where(box_lane == box, pair_value, 0.0)
        value += table[0:8] + table[8:16] + table[16:24]
    g_sum[0] = jnp.sum(value, axis=0, keepdims=True)

    g_all = [
        [
            remote(
                g_sum.at[stage],
                g_got.at[stage, place],
                g_s.at[stage, place],
                g_r.at[stage, place],
                device,
            )
            for place, device in groups[stage]
        ]
        for stage in range(3)
    ]

    def g_gather(stage):
        total = g_sum[stage]
        for (place, _), copy in zip(groups[stage], g_all[stage]):
            copy.wait_recv()
            total = total + g_got[stage, place]
        return total

    for copy in g_all[0]:
        copy.start()
    pass_sums(1)
    g_sum[1] = g_gather(0)
    for copy in g_all[1]:
        copy.start()

    for copy in fars:
        copy.wait_recv()
    far = far_sum[...]
    for k in range(1, NZ):
        far = far + far_got[k]
    far = far * norm_far
    far_re = jnp.broadcast_to(far[:, 0:1], (16, 128))
    far_im = jnp.broadcast_to(far[:, 64:65], (16, 128))

    def finish(h):
        for way in (0, 1):
            part_copies[way, 1, h].wait_recv()
        for c in range(h * half, (h + 1) * half):
            re = pl.ds(2 * c, 16, stride=16)
            im = pl.ds(2 * c + 1, 16, stride=16)
            rr, ri = rad[re, :], rad[im, :]
            total = (own_sum[c] + (part_got[0, 0, c] + part_got[1, 0, c])).reshape(32, 128)
            res_re = ((far_re * rr + far_im * ri) - total[0:16]).astype(BF16)
            res_im = ((far_im * rr - far_re * ri) - total[16:32]).astype(BF16)
            lhs[c, 0:16, 0:128] = res_re
            lhs[c, 0:16, 128:256] = res_im
            lhs[c, 16:32, 0:128] = res_im
            lhs[c, 16:32, 128:256] = -res_re
            update = jnp.dot(lhs[c], inv[c], preferred_element_type=F32)
            out[re, :] = adj[re, :] + update[0:16]
            out[im, :] = adj[im, :] + update[16:32]

    inv_in.wait()
    finish(0)
    g_sum[2] = g_gather(1)
    for copy in g_all[2]:
        copy.start()
    finish(1)
    for copy in msgs + fars + g_all[0] + g_all[1]:
        copy.wait_send()
    for copy in list(cur_copies.values()) + list(part_copies.values()):
        copy.wait_send()
    for place in (0, 1, 2, 3, 4, 5, 6, 7):
        terms_gone(place)
    total = g_gather(2)
    for i in range(BOX_DEV):
        mine = lane[0:1] == b * BOX_DEV + i
        grad[:, i : i + 1] = jnp.sum(jnp.where(mine, total, 0.0), axis=1, keepdims=True) * grad_norm

    for copy in g_all[2]:
        copy.wait_send()


def on_device(
    adjoint,
    currents,
    radiation,
    near_blocks,
    inverse_blocks,
    col_device,
    col_offset,
    box_of_block,
    pair_rate,
):
    angles_here, blocks, unknowns = adjoint.shape[1], adjoint.shape[2], adjoint.shape[4]
    near_count = near_blocks.shape[1]
    pairs = blocks * near_count
    ny, nc = lax.axis_size("angle"), lax.axis_size("pol")
    basis_count = lax.axis_size("basis")
    rows = angles_here * blocks * 2

    vmem = pl.BlockSpec(memory_space=pltpu.VMEM)
    dma = pltpu.SemaphoreType.DMA
    sizes = (
        ny,
        nc,
        1.0 / math.sqrt(blocks * basis_count * unknowns),
        -1.0 / math.sqrt(4 * unknowns * angles_here * ny * near_count),
    )
    out, grad = pl.pallas_call(
        functools.partial(kernel, sizes),
        out_shape=(
            jax.ShapeDtypeStruct((rows, unknowns), F32),
            jax.ShapeDtypeStruct((1, BOX_DEV), F32),
        ),
        in_specs=[pl.BlockSpec(memory_space=pltpu.HBM)] * 9,
        out_specs=(vmem, vmem),
        scratch_shapes=[
            pltpu.SMEM((blocks,), jnp.int32),
            pltpu.VMEM((blocks, near_count), jnp.int32),
            pltpu.VMEM((blocks, near_count), jnp.int32),
            pltpu.VMEM((blocks, near_count), F32),
            pltpu.VMEM((rows, unknowns), F32),
            pltpu.VMEM((rows, unknowns), F32),
            pltpu.VMEM((rows, unknowns), F32),
            pltpu.VMEM((pairs, 2 * unknowns, unknowns), BF16),
            pltpu.VMEM((blocks, 2 * unknowns, unknowns), BF16),
            pltpu.VMEM((8, 128), jnp.int32),
            pltpu.SMEM((8, 128), jnp.int32),
            pltpu.VMEM((blocks, 32, 256), BF16),
            pltpu.VMEM((NZ, NX - 1, CAP, 4, 8, 128), F32),
            pltpu.VMEM((NZ, NX, CAP, 4, 8, 128), F32),
            pltpu.VMEM((NZ, blocks, 4, 8, 128), F32),
            pltpu.VMEM((2, 4, blocks, 4, 8, 128), F32),
            pltpu.VMEM((2, 4, blocks, 4, 8, 128), F32),
            pltpu.VMEM((blocks, 4, 8, 128), F32),
            pltpu.VMEM((NX, 64, 128), F32),
            pltpu.VMEM((NX, 64, 128), F32),
            pltpu.VMEM((16, 128), F32),
            pltpu.VMEM((NZ, 16, 128), F32),
            pltpu.VMEM((NX, NZ * CAP, 128), F32),
            pltpu.VMEM((3, 1, 128), F32),
            pltpu.VMEM((3, 8, 1, 128), F32),
            dma((10,)),
            dma((NZ, NX - 1)),
            dma((NZ, NX - 1)),
            dma((2, 4, 2)),
            dma((2, 4, 2)),
            dma((2, 4, 2)),
            dma((2, 4, 2)),
            dma((NX,)),
            dma((NX,)),
            dma((NZ,)),
            dma((NZ,)),
            dma((3, 8)),
            dma((3, 8)),
        ],
        compiler_params=pltpu.CompilerParams(
            collective_id=0, has_side_effects=True, vmem_limit_bytes=40 << 20
        ),
        name="sweep",
    )(*[pltpu.with_memory_space_constraint(a, pltpu.HBM) for a in (
        box_of_block,
        col_device,
        col_offset,
        pair_rate,
        adjoint.reshape(rows, unknowns),
        currents.reshape(rows, unknowns),
        radiation.reshape(rows, unknowns),
        near_blocks.reshape(pairs, 2 * unknowns, unknowns),
        inverse_blocks.reshape(blocks, 2 * unknowns, unknowns),
    )])
    return (out.reshape(adjoint.shape), grad.reshape(BOX_DEV))


def solution(mesh):
    placed = (
        P("pol", "angle", "basis", None, None),
        P("pol", "angle", "basis", None, None),
        P("pol", "angle", "basis", None, None),
        P("basis", None, None, None, None),
        P("basis", None, None, None),
        P("basis", None),
        P("basis", None),
        P("basis"),
        P("basis", None),
    )
    return jax.shard_map(
        on_device,
        mesh=mesh,
        in_specs=placed,
        out_specs=(P("pol", "angle", "basis", None, None), P("basis")),
        check_vma=False,
    )
```

```python
import functools
import math

import jax
import jax.numpy as jnp
from jax import lax
from jax.experimental import pallas as pl
from jax.experimental.pallas import tpu as pltpu
from jax.sharding import PartitionSpec as P

MESH = pl.DeviceIdType.MESH
F32 = jnp.float32
BF16 = jnp.bfloat16

NX, NZ = 4, 8
CAP = 3
BOX_DEV = 4
ORDER = (4, 3, 5, 2, 6, 1, 7, 0)
PLACE = {distance % NZ: place for place, distance in enumerate(ORDER)}


def kernel(
    sizes,
    box_hbm,
    dev_hbm,
    off_hbm,
    rate_hbm,
    adj_hbm,
    cur_hbm,
    rad_hbm,
    near_hbm,
    inv_hbm,
    out,
    grad,
    box_of,
    dev,
    off_of,
    rate_of,
    adj,
    cur,
    rad,
    near,
    inv,
    tab_v,
    pair_tab,
    lhs,
    sent,
    got,
    cur_at,
    part,
    part_got,
    own_sum,
    msg,
    msg_got,
    far_sum,
    far_got,
    lane_dots,
    g_sum,
    g_got,
    local_sem,
    term_s,
    term_r,
    cur_s,
    cur_r,
    part_s,
    part_r,
    msg_s,
    msg_r,
    far_s,
    far_r,
    g_s,
    g_r,
):
    ny, nc, norm_far, grad_norm = sizes
    blocks, near_count = 8, 6
    pairs = blocks * near_count
    half = blocks // 2
    b = lax.axis_index("basis")
    y = lax.axis_index("angle")
    c0 = lax.axis_index("pol")
    x = lax.div(b, NZ)
    z = lax.rem(b, NZ)

    def at(dx=0, dz=0, dy=0, dc=0):
        basis = lax.rem(x + dx, NX) * NZ + lax.rem(z + dz, NZ)
        return (basis, lax.rem(y + dy, ny), lax.rem(c0 + dc, nc))

    def remote(src, dst, send_sem, recv_sem, device):
        return pltpu.make_async_remote_copy(
            src_ref=src,
            dst_ref=dst,
            send_sem=send_sem,
            recv_sem=recv_sem,
            device_id=device,
            device_id_type=MESH,
        )

    loads = [
        pltpu.make_async_copy(src, dst, local_sem.at[i])
        for i, (src, dst) in enumerate(
            [
                (box_hbm, box_of),
                (dev_hbm, dev),
                (off_hbm, off_of),
                (rate_hbm, rate_of),
                (cur_hbm, cur),
                (adj_hbm, adj),
                (rad_hbm, rad),
                (near_hbm, near),
                (inv_hbm, inv),
            ]
        )
    ]
    for copy in loads:
        copy.start()
    box_in, dev_in, off_in, rate_in, cur_in, adj_in, rad_in, near_in, inv_in = loads

    groups = [
        [(dx * nc + dc, at(dx=dx, dc=dc)) for dx in range(NX) for dc in range(nc) if dx or dc],
        [(dz, at(dz=dz)) for dz in range(1, NZ)],
        [(dy, at(dy=dy)) for dy in range(1, ny)],
    ]
    barrier = pltpu.get_barrier_semaphore()
    for group in groups:
        for _, device in group:
            pl.semaphore_signal(barrier, inc=1, device_id=device, device_id_type=MESH)

    for copy in (box_in, dev_in, off_in, rate_in):
        copy.wait()

    def column(values):
        return jnp.concatenate(
            [jnp.broadcast_to(values[:, k : k + 1], (blocks, 128)) for k in range(near_count)]
        )

    sub = lax.broadcasted_iota(jnp.int32, (pairs, 128), 0)
    lane = lax.broadcasted_iota(jnp.int32, (pairs, 128), 1)
    target = column(dev[...].astype(F32))
    target_row = jnp.sum(jnp.where(sub == lane, target, 0.0), axis=0, keepdims=True)
    rank = jnp.sum(
        jnp.where((target == target_row) & (sub < lane), 1.0, 0.0), axis=0, keepdims=True
    )
    device_row = target_row.astype(jnp.int32)
    far_x = (lax.shift_right_logical(device_row, 3) + (NX - x)) & (NX - 1)
    far_z = ((device_row & (NZ - 1)) + (NZ - z)) & (NZ - 1)
    place_row = jnp.zeros((1, 128), jnp.int32)
    for place, distance in enumerate(ORDER):
        place_row = jnp.where(far_z == distance, place, place_row)
    slot_row = ((far_x * NZ + place_row) * CAP).astype(F32) + rank
    slot_row = jnp.where(lane[0:1] < pairs, slot_row, -1.0)
    slot_col = jnp.sum(jnp.where(sub == lane, slot_row, 0.0), axis=1, keepdims=True)
    pair_id = ((sub & (blocks - 1)) * near_count + lax.shift_right_logical(sub, 3)).astype(F32)
    pair_row = jnp.sum(
        jnp.where(slot_col == lane.astype(F32), pair_id, 0.0), axis=0, keepdims=True
    )
    tab_v[...] = jnp.broadcast_to(pair_row, (8, 128)).astype(jnp.int32)
    tab_copy = pltpu.make_async_copy(tab_v, pair_tab, local_sem.at[9])
    tab_copy.start()

    slots = NX * NZ * CAP
    hot = jnp.where(
        slot_row == lax.broadcasted_iota(jnp.int32, (slots, 128), 0).astype(F32), 1.0, 0.0
    )
    rest = jnp.zeros((128 - pairs, 128), F32)
    off_col = jnp.concatenate([column(off_of[...].astype(F32)) + 1.0, rest])
    off_tab = (
        jnp.dot(hot.astype(BF16), off_col.astype(BF16), preferred_element_type=F32) - 1.0
    )
    row = lax.broadcasted_iota(jnp.int32, (blocks, 128), 0)
    box = jnp.zeros((blocks, 128), F32)
    for r in range(blocks):
        box = jnp.where(row == r, box_of[r].astype(F32), box)
    rate_box = jnp.where(
        lane < 64, column(rate_of[...]), jnp.concatenate([box] * near_count)
    )
    rate_box = jnp.dot(
        hot,
        jnp.concatenate([rate_box, rest]),
        precision=lax.Precision.HIGHEST,
        preferred_element_type=F32,
    )

    cur_in.wait()
    for r in range(blocks):
        re = pl.ds(2 * r, 16, stride=16)
        im = pl.ds(2 * r + 1, 16, stride=16)
        cur_at[PLACE[0], r, 0:2] = cur[re, :].reshape(2, 8, 128)
        cur_at[PLACE[0], r, 2:4] = cur[im, :].reshape(2, 8, 128)
    adj_in.wait()
    for r in range(blocks):
        re = pl.ds(2 * r, 16, stride=16)
        im = pl.ds(2 * r + 1, 16, stride=16)
        ar, ai = adj[re, :].astype(BF16), adj[im, :].astype(BF16)
        lhs[r, 0:16, 0:128] = ar
        lhs[r, 0:16, 128:256] = ai
        lhs[r, 16:32, 0:128] = ai
        lhs[r, 16:32, 128:256] = -ar
    rad_in.wait()
    far_re = jnp.zeros((16, 128), F32)
    far_im = jnp.zeros((16, 128), F32)
    for r in range(blocks):
        re = pl.ds(2 * r, 16, stride=16)
        im = pl.ds(2 * r + 1, 16, stride=16)
        rr, ri = rad[re, :], rad[im, :]
        cr, ci = cur[re, :], cur[im, :]
        far_re += rr * cr - ri * ci
        far_im += rr * ci + ri * cr
    far_tile = jnp.where(
        lane[0:16] < 64,
        jnp.sum(far_re, axis=1, keepdims=True),
        jnp.sum(far_im, axis=1, keepdims=True),
    )
    for k in range(NX):
        to = msg if k else msg_got
        rows = slice(k * NZ * CAP, (k + 1) * NZ * CAP)
        to[k, 0:16] = far_tile
        to[k, 16:40] = off_tab[rows]
        to[k, 40:64] = rate_box[rows]
    tab_copy.wait()
    near_in.wait()

    pl.semaphore_wait(barrier, sum(len(group) for group in groups))

    def halves(hops, way):
        return (0, 1) if hops < 4 else (way,)

    def cur_copy(way, step, h):
        sign = 1 if way == 0 else -1
        rows = slice(h * half, (h + 1) * half)
        return remote(
            cur_at.at[PLACE[(-sign * (step - 1)) % NZ], rows],
            cur_at.at[PLACE[(-sign * step) % NZ], rows],
            cur_s.at[way, step - 1, h],
            cur_r.at[way, step - 1, h],
            at(dz=sign % NZ),
        )

    cur_copies = {
        (way, step, h): cur_copy(way, step, h)
        for way in (0, 1)
        for step in range(1, 5)
        for h in halves(step, way)
    }

    def pass_currents(step, h):
        for way in (0, 1):
            cur_copies[way, step - 1, h].wait_recv()
            if h in halves(step, way):
                cur_copies[way, step, h].start()

    for h in (0, 1):
        for way in (0, 1):
            cur_copies[way, 1, h].start()

    def term_copy(place, k):
        return remote(
            sent.at[place, k - 1],
            got.at[place, k],
            term_s.at[place, k - 1],
            term_r.at[place, k - 1],
            at(dx=k),
        )

    def send_terms(place):
        for k in (2, 1, 3, 0):
            for s in range(CAP):
                pair = pair_tab[0, k * NZ * CAP + place * CAP + s]
                pair = jnp.clip(pair, 0, pairs - 1)
                term = jnp.dot(
                    lhs[lax.div(pair, near_count)], near[pair], preferred_element_type=F32
                ).reshape(4, 8, 128)
                if k:
                    sent[place, k - 1, s] = term
                else:
                    got[place, 0, s] = term
            if k:
                term_copy(place, k).start()

    def terms_gone(place):
        for k in range(1, NX):
            term_copy(place, k).wait_send()

    def masks(place, k, s):
        at_row = 16 + place * CAP + s
        off = jnp.broadcast_to(msg_got[k, at_row : at_row + 1, :], (8, 128))
        return [(off == float(c))[None] for c in range(blocks)]

    def arrive(*places):
        for place in places:
            for k in range(1, NX):
                term_copy(place, k).wait_recv()

    def combine(place, to):
        sums = [jnp.zeros((4, 8, 128), F32) for _ in range(blocks)]
        for k in range(NX):
            for s in range(CAP):
                term = got[place, k, s]
                for c, mask in enumerate(masks(place, k, s)):
                    sums[c] = sums[c] + jnp.where(mask, term, 0.0)
        for c in range(blocks):
            to(c)[...] = sums[c]

    def dots(place):
        for k in range(NX):
            for s in range(CAP):
                chosen = jnp.zeros((4, 8, 128), F32)
                for c, mask in enumerate(masks(place, k, s)):
                    chosen = jnp.where(mask, cur_at[place, c], chosen)
                product = jnp.sum(got[place, k, s] * chosen, axis=0)
                lane_dots[k, place * CAP + s : place * CAP + s + 1, :] = jnp.sum(
                    product, axis=0, keepdims=True
                )

    def part_copy(way, hops, h):
        rows = slice(h * half, (h + 1) * half)
        return remote(
            part.at[way, hops - 1, rows],
            part_got.at[way, hops - 1, rows],
            part_s.at[way, hops - 1, h],
            part_r.at[way, hops - 1, h],
            at(dz=1 if way == 0 else NZ - 1),
        )

    part_copies = {
        (way, hops, h): part_copy(way, hops, h)
        for way in (0, 1)
        for hops in range(1, 5)
        for h in halves(hops, way)
    }

    def combine_ring(hops):
        if hops == 4:
            combine(PLACE[4], lambda c: part.at[c // half, 3, c])
        else:
            combine(PLACE[hops], lambda c: part.at[0, hops - 1, c])
            combine(PLACE[NZ - hops], lambda c: part.at[1, hops - 1, c])

    def pass_sums(hops):
        for h in (0, 1):
            for way in (0, 1):
                if h in halves(hops + 1, way):
                    part_copies[way, hops + 1, h].wait_recv()
                    for c in range(h * half, (h + 1) * half):
                        part[way, hops - 1, c] += part_got[way, hops, c]
                part_copies[way, hops, h].start()

    msgs = [
        remote(msg.at[k], msg_got.at[k], msg_s.at[k], msg_r.at[k], at(dx=k))
        for k in range(1, NX)
    ]
    for copy in msgs:
        copy.start()
    send_terms(0)
    send_terms(1)
    pass_currents(2, 0)
    send_terms(2)
    pass_currents(2, 1)
    send_terms(3)
    for copy in msgs:
        copy.wait_recv()
    arrive(PLACE[4])
    combine_ring(4)
    for way in (0, 1):
        part_copies[way, 4, way].start()
    pass_currents(3, 0)
    send_terms(4)
    pass_currents(3, 1)
    far_sum[...] = msg_got[0, 0:16] + msg_got[1, 0:16] + msg_got[2, 0:16] + msg_got[3, 0:16]
    fars = [
        remote(far_sum, far_got.at[k], far_s.at[k], far_r.at[k], at(dz=k)) for k in range(1, NZ)
    ]
    for copy in fars:
        copy.start()
    arrive(PLACE[3], PLACE[5])
    combine_ring(3)
    pass_sums(3)
    send_terms(5)
    pass_currents(4, 0)
    send_terms(6)
    pass_currents(4, 1)
    send_terms(7)
    arrive(PLACE[2], PLACE[6])
    combine_ring(2)
    pass_sums(2)
    arrive(PLACE[1], PLACE[7])
    dots(PLACE[1])
    dots(PLACE[7])
    dots(PLACE[2])
    dots(PLACE[6])
    dots(PLACE[3])
    dots(PLACE[5])
    for way in (0, 1):
        cur_copies[way, 4, way].wait_recv()
    dots(PLACE[4])
    arrive(PLACE[0])
    dots(PLACE[0])

    value = jnp.zeros((8, 128), F32)
    box_lane = lax.broadcasted_iota(jnp.int32, (NZ * CAP, 128), 1).astype(F32)
    for k in range(NX):
        rate = msg_got[k, 40:64, 0:1]
        box = msg_got[k, 40:64, 64:65]
        pair_value = rate * jnp.sum(lane_dots[k], axis=1, keepdims=True)
        table = jnp.where(box_lane == box, pair_value, 0.0)
        value += table[0:8] + table[8:16] + table[16:24]
    g_sum[0] = jnp.sum(value, axis=0, keepdims=True)

    g_all = [
        [
            remote(
                g_sum.at[stage],
                g_got.at[stage, place],
                g_s.at[stage, place],
                g_r.at[stage, place],
                device,
            )
            for place, device in groups[stage]
        ]
        for stage in range(3)
    ]

    def g_gather(stage):
        total = g_sum[stage]
        for (place, _), copy in zip(groups[stage], g_all[stage]):
            copy.wait_recv()
            total = total + g_got[stage, place]
        return total

    for copy in g_all[0]:
        copy.start()
    combine_ring(1)
    pass_sums(1)
    combine(PLACE[0], lambda c: own_sum.at[c])
    g_sum[1] = g_gather(0)
    for copy in g_all[1]:
        copy.start()

    for copy in fars:
        copy.wait_recv()
    far = far_sum[...]
    for k in range(1, NZ):
        far = far + far_got[k]
    far = far * norm_far
    far_re = jnp.broadcast_to(far[:, 0:1], (16, 128))
    far_im = jnp.broadcast_to(far[:, 64:65], (16, 128))

    def finish(h):
        for way in (0, 1):
            part_copies[way, 1, h].wait_recv()
        for c in range(h * half, (h + 1) * half):
            re = pl.ds(2 * c, 16, stride=16)
            im = pl.ds(2 * c + 1, 16, stride=16)
            rr, ri = rad[re, :], rad[im, :]
            total = (own_sum[c] + (part_got[0, 0, c] + part_got[1, 0, c])).reshape(32, 128)
            res_re = ((far_re * rr + far_im * ri) - total[0:16]).astype(BF16)
            res_im = ((far_im * rr - far_re * ri) - total[16:32]).astype(BF16)
            lhs[c, 0:16, 0:128] = res_re
            lhs[c, 0:16, 128:256] = res_im
            lhs[c, 16:32, 0:128] = res_im
            lhs[c, 16:32, 128:256] = -res_re
            update = jnp.dot(lhs[c], inv[c], preferred_element_type=F32)
            out[re, :] = adj[re, :] + update[0:16]
            out[im, :] = adj[im, :] + update[16:32]

    inv_in.wait()
    finish(0)
    g_sum[2] = g_gather(1)
    for copy in g_all[2]:
        copy.start()
    finish(1)
    for copy in msgs + fars + g_all[0] + g_all[1]:
        copy.wait_send()
    for copy in list(cur_copies.values()) + list(part_copies.values()):
        copy.wait_send()
    for place in (0, 1, 2, 3, 4, 5, 6, 7):
        terms_gone(place)
    total = g_gather(2)
    for i in range(BOX_DEV):
        mine = lane[0:1] == b * BOX_DEV + i
        grad[:, i : i + 1] = jnp.sum(jnp.where(mine, total, 0.0), axis=1, keepdims=True) * grad_norm

    for copy in g_all[2]:
        copy.wait_send()


def on_device(
    adjoint,
    currents,
    radiation,
    near_blocks,
    inverse_blocks,
    col_device,
    col_offset,
    box_of_block,
    pair_rate,
):
    angles_here, blocks, unknowns = adjoint.shape[1], adjoint.shape[2], adjoint.shape[4]
    near_count = near_blocks.shape[1]
    pairs = blocks * near_count
    ny, nc = lax.axis_size("angle"), lax.axis_size("pol")
    basis_count = lax.axis_size("basis")
    rows = angles_here * blocks * 2

    vmem = pl.BlockSpec(memory_space=pltpu.VMEM)
    dma = pltpu.SemaphoreType.DMA
    sizes = (
        ny,
        nc,
        1.0 / math.sqrt(blocks * basis_count * unknowns),
        -1.0 / math.sqrt(4 * unknowns * angles_here * ny * near_count),
    )
    out, grad = pl.pallas_call(
        functools.partial(kernel, sizes),
        out_shape=(
            jax.ShapeDtypeStruct((rows, unknowns), F32),
            jax.ShapeDtypeStruct((1, BOX_DEV), F32),
        ),
        in_specs=[pl.BlockSpec(memory_space=pltpu.HBM)] * 9,
        out_specs=(vmem, vmem),
        scratch_shapes=[
            pltpu.SMEM((blocks,), jnp.int32),
            pltpu.VMEM((blocks, near_count), jnp.int32),
            pltpu.VMEM((blocks, near_count), jnp.int32),
            pltpu.VMEM((blocks, near_count), F32),
            pltpu.VMEM((rows, unknowns), F32),
            pltpu.VMEM((rows, unknowns), F32),
            pltpu.VMEM((rows, unknowns), F32),
            pltpu.VMEM((pairs, 2 * unknowns, unknowns), BF16),
            pltpu.VMEM((blocks, 2 * unknowns, unknowns), BF16),
            pltpu.VMEM((8, 128), jnp.int32),
            pltpu.SMEM((8, 128), jnp.int32),
            pltpu.VMEM((blocks, 32, 256), BF16),
            pltpu.VMEM((NZ, NX - 1, CAP, 4, 8, 128), F32),
            pltpu.VMEM((NZ, NX, CAP, 4, 8, 128), F32),
            pltpu.VMEM((NZ, blocks, 4, 8, 128), F32),
            pltpu.VMEM((2, 4, blocks, 4, 8, 128), F32),
            pltpu.VMEM((2, 4, blocks, 4, 8, 128), F32),
            pltpu.VMEM((blocks, 4, 8, 128), F32),
            pltpu.VMEM((NX, 64, 128), F32),
            pltpu.VMEM((NX, 64, 128), F32),
            pltpu.VMEM((16, 128), F32),
            pltpu.VMEM((NZ, 16, 128), F32),
            pltpu.VMEM((NX, NZ * CAP, 128), F32),
            pltpu.VMEM((3, 1, 128), F32),
            pltpu.VMEM((3, 8, 1, 128), F32),
            dma((10,)),
            dma((NZ, NX - 1)),
            dma((NZ, NX - 1)),
            dma((2, 4, 2)),
            dma((2, 4, 2)),
            dma((2, 4, 2)),
            dma((2, 4, 2)),
            dma((NX,)),
            dma((NX,)),
            dma((NZ,)),
            dma((NZ,)),
            dma((3, 8)),
            dma((3, 8)),
        ],
        compiler_params=pltpu.CompilerParams(
            collective_id=0, has_side_effects=True, vmem_limit_bytes=40 << 20
        ),
        name="sweep",
    )(*[pltpu.with_memory_space_constraint(a, pltpu.HBM) for a in (
        box_of_block,
        col_device,
        col_offset,
        pair_rate,
        adjoint.reshape(rows, unknowns),
        currents.reshape(rows, unknowns),
        radiation.reshape(rows, unknowns),
        near_blocks.reshape(pairs, 2 * unknowns, unknowns),
        inverse_blocks.reshape(blocks, 2 * unknowns, unknowns),
    )])
    return (out.reshape(adjoint.shape), grad.reshape(BOX_DEV))


def solution(mesh):
    placed = (
        P("pol", "angle", "basis", None, None),
        P("pol", "angle", "basis", None, None),
        P("pol", "angle", "basis", None, None),
        P("basis", None, None, None, None),
        P("basis", None, None, None),
        P("basis", None),
        P("basis", None),
        P("basis"),
        P("basis", None),
    )
    return jax.shard_map(
        on_device,
        mesh=mesh,
        in_specs=placed,
        out_specs=(P("pol", "angle", "basis", None, None), P("basis")),
        check_vma=False,
    )
```

```python
import functools
import math

import jax
import jax.numpy as jnp
from jax import lax
from jax.experimental import pallas as pl
from jax.experimental.pallas import tpu as pltpu
from jax.sharding import PartitionSpec as P

MESH = pl.DeviceIdType.MESH
F32 = jnp.float32
BF16 = jnp.bfloat16

NX, NZ = 4, 8
CAP = 3
BOX_DEV = 4
ORDER = (4, 3, 5, 2, 6, 1, 7, 0)
PLACE = {distance % NZ: place for place, distance in enumerate(ORDER)}


def kernel(
    sizes,
    box_hbm,
    dev_hbm,
    off_hbm,
    rate_hbm,
    adj_hbm,
    cur_hbm,
    rad_hbm,
    near_hbm,
    inv_hbm,
    out,
    grad,
    box_of,
    dev,
    off_of,
    rate_of,
    adj,
    cur,
    rad,
    near,
    inv,
    tab_v,
    pair_tab,
    lhs,
    sent,
    got,
    cur_at,
    part,
    part_got,
    own_sum,
    msg,
    msg_got,
    far_sum,
    far_got,
    lane_dots,
    g_sum,
    g_got,
    local_sem,
    term_s,
    term_r,
    cur_s,
    cur_r,
    part_s,
    part_r,
    msg_s,
    msg_r,
    far_s,
    far_r,
    g_s,
    g_r,
):
    ny, nc, norm_far, grad_norm = sizes
    blocks, near_count = 8, 6
    pairs = blocks * near_count
    half = blocks // 2
    b = lax.axis_index("basis")
    y = lax.axis_index("angle")
    c0 = lax.axis_index("pol")
    x = lax.div(b, NZ)
    z = lax.rem(b, NZ)

    def at(dx=0, dz=0, dy=0, dc=0):
        basis = lax.rem(x + dx, NX) * NZ + lax.rem(z + dz, NZ)
        return (basis, lax.rem(y + dy, ny), lax.rem(c0 + dc, nc))

    def remote(src, dst, send_sem, recv_sem, device):
        return pltpu.make_async_remote_copy(
            src_ref=src,
            dst_ref=dst,
            send_sem=send_sem,
            recv_sem=recv_sem,
            device_id=device,
            device_id_type=MESH,
        )

    loads = [
        pltpu.make_async_copy(src, dst, local_sem.at[i])
        for i, (src, dst) in enumerate(
            [
                (box_hbm, box_of),
                (dev_hbm, dev),
                (off_hbm, off_of),
                (rate_hbm, rate_of),
                (cur_hbm, cur),
                (adj_hbm, adj),
                (rad_hbm, rad),
                (near_hbm, near),
                (inv_hbm, inv),
            ]
        )
    ]
    for copy in loads:
        copy.start()
    box_in, dev_in, off_in, rate_in, cur_in, adj_in, rad_in, near_in, inv_in = loads

    groups = [
        [(dx * nc + dc, at(dx=dx, dc=dc)) for dx in range(NX) for dc in range(nc) if dx or dc],
        [(dz, at(dz=dz)) for dz in range(1, NZ)],
        [(dy, at(dy=dy)) for dy in range(1, ny)],
    ]
    barrier = pltpu.get_barrier_semaphore()
    for group in groups:
        for _, device in group:
            pl.semaphore_signal(barrier, inc=1, device_id=device, device_id_type=MESH)

    for copy in (box_in, dev_in, off_in, rate_in):
        copy.wait()

    def column(values):
        return jnp.concatenate(
            [jnp.broadcast_to(values[:, k : k + 1], (blocks, 128)) for k in range(near_count)]
        )

    sub = lax.broadcasted_iota(jnp.int32, (pairs, 128), 0)
    lane = lax.broadcasted_iota(jnp.int32, (pairs, 128), 1)
    target = column(dev[...].astype(F32))
    target_row = jnp.sum(jnp.where(sub == lane, target, 0.0), axis=0, keepdims=True)
    rank = jnp.sum(
        jnp.where((target == target_row) & (sub < lane), 1.0, 0.0), axis=0, keepdims=True
    )
    device_row = target_row.astype(jnp.int32)
    far_x = (lax.shift_right_logical(device_row, 3) + (NX - x)) & (NX - 1)
    far_z = ((device_row & (NZ - 1)) + (NZ - z)) & (NZ - 1)
    place_row = jnp.zeros((1, 128), jnp.int32)
    for place, distance in enumerate(ORDER):
        place_row = jnp.where(far_z == distance, place, place_row)
    slot_row = ((far_x * NZ + place_row) * CAP).astype(F32) + rank
    slot_row = jnp.where(lane[0:1] < pairs, slot_row, -1.0)
    slot_col = jnp.sum(jnp.where(sub == lane, slot_row, 0.0), axis=1, keepdims=True)
    pair_id = ((sub & (blocks - 1)) * near_count + lax.shift_right_logical(sub, 3)).astype(F32)
    pair_row = jnp.sum(
        jnp.where(slot_col == lane.astype(F32), pair_id, 0.0), axis=0, keepdims=True
    )
    tab_v[...] = jnp.broadcast_to(pair_row, (8, 128)).astype(jnp.int32)
    tab_copy = pltpu.make_async_copy(tab_v, pair_tab, local_sem.at[9])
    tab_copy.start()

    slots = NX * NZ * CAP
    hot = jnp.where(
        slot_row == lax.broadcasted_iota(jnp.int32, (slots, 128), 0).astype(F32), 1.0, 0.0
    )
    rest = jnp.zeros((128 - pairs, 128), F32)
    off_col = jnp.concatenate([column(off_of[...].astype(F32)) + 1.0, rest])
    off_tab = (
        jnp.dot(hot.astype(BF16), off_col.astype(BF16), preferred_element_type=F32) - 1.0
    )
    row = lax.broadcasted_iota(jnp.int32, (blocks, 128), 0)
    box = jnp.zeros((blocks, 128), F32)
    for r in range(blocks):
        box = jnp.where(row == r, box_of[r].astype(F32), box)
    rate_box = jnp.where(
        lane < 64, column(rate_of[...]), jnp.concatenate([box] * near_count)
    )
    rate_box = jnp.dot(
        hot,
        jnp.concatenate([rate_box, rest]),
        precision=lax.Precision.HIGHEST,
        preferred_element_type=F32,
    )

    cur_in.wait()
    for r in range(blocks):
        re = pl.ds(2 * r, 16, stride=16)
        im = pl.ds(2 * r + 1, 16, stride=16)
        cur_at[PLACE[0], r, 0:2] = cur[re, :].reshape(2, 8, 128)
        cur_at[PLACE[0], r, 2:4] = cur[im, :].reshape(2, 8, 128)
    adj_in.wait()
    for r in range(blocks):
        re = pl.ds(2 * r, 16, stride=16)
        im = pl.ds(2 * r + 1, 16, stride=16)
        ar, ai = adj[re, :].astype(BF16), adj[im, :].astype(BF16)
        lhs[r, 0:16, 0:128] = ar
        lhs[r, 0:16, 128:256] = ai
        lhs[r, 16:32, 0:128] = ai
        lhs[r, 16:32, 128:256] = -ar
    rad_in.wait()
    far_re = jnp.zeros((16, 128), F32)
    far_im = jnp.zeros((16, 128), F32)
    for r in range(blocks):
        re = pl.ds(2 * r, 16, stride=16)
        im = pl.ds(2 * r + 1, 16, stride=16)
        rr, ri = rad[re, :], rad[im, :]
        cr, ci = cur[re, :], cur[im, :]
        far_re += rr * cr - ri * ci
        far_im += rr * ci + ri * cr
    far_tile = jnp.where(
        lane[0:16] < 64,
        jnp.sum(far_re, axis=1, keepdims=True),
        jnp.sum(far_im, axis=1, keepdims=True),
    )
    for k in range(NX):
        to = msg if k else msg_got
        rows = slice(k * NZ * CAP, (k + 1) * NZ * CAP)
        to[k, 0:16] = far_tile
        to[k, 16:40] = off_tab[rows]
        to[k, 40:64] = rate_box[rows]
    tab_copy.wait()
    near_in.wait()

    pl.semaphore_wait(barrier, sum(len(group) for group in groups))

    def halves(hops, way):
        return (0, 1) if hops < 4 else (way,)

    def cur_copy(way, step, h):
        sign = 1 if way == 0 else -1
        rows = slice(h * half, (h + 1) * half)
        return remote(
            cur_at.at[PLACE[(-sign * (step - 1)) % NZ], rows],
            cur_at.at[PLACE[(-sign * step) % NZ], rows],
            cur_s.at[way, step - 1, h],
            cur_r.at[way, step - 1, h],
            at(dz=sign % NZ),
        )

    cur_copies = {
        (way, step, h): cur_copy(way, step, h)
        for way in (0, 1)
        for step in range(1, 5)
        for h in halves(step, way)
    }

    def pass_currents(step, h):
        for way in (0, 1):
            cur_copies[way, step - 1, h].wait_recv()
            if h in halves(step, way):
                cur_copies[way, step, h].start()

    for h in (0, 1):
        for way in (0, 1):
            cur_copies[way, 1, h].start()

    def term_copy(place, k):
        return remote(
            sent.at[place, k - 1],
            got.at[place, k],
            term_s.at[place, k - 1],
            term_r.at[place, k - 1],
            at(dx=k),
        )

    def send_terms(place):
        for k in (2, 1, 3, 0):
            for s in range(CAP):
                pair = pair_tab[0, k * NZ * CAP + place * CAP + s]
                pair = jnp.clip(pair, 0, pairs - 1)
                term = jnp.dot(
                    lhs[lax.div(pair, near_count)], near[pair], preferred_element_type=F32
                ).reshape(4, 8, 128)
                if k:
                    sent[place, k - 1, s] = term
                else:
                    got[place, 0, s] = term
            if k:
                term_copy(place, k).start()

    def terms_gone(place):
        for k in range(1, NX):
            term_copy(place, k).wait_send()

    def masks(place, k, s):
        at_row = 16 + place * CAP + s
        off = jnp.broadcast_to(msg_got[k, at_row : at_row + 1, :], (8, 128))
        return [(off == float(c))[None] for c in range(blocks)]

    def arrive(*places):
        for place in places:
            for k in range(1, NX):
                term_copy(place, k).wait_recv()

    def combine(place, to):
        sums = [jnp.zeros((4, 8, 128), F32) for _ in range(blocks)]
        for k in range(NX):
            for s in range(CAP):
                term = got[place, k, s]
                for c, mask in enumerate(masks(place, k, s)):
                    sums[c] = sums[c] + jnp.where(mask, term, 0.0)
        for c in range(blocks):
            to(c)[...] = sums[c]

    def dots(place):
        for k in range(NX):
            for s in range(CAP):
                chosen = jnp.zeros((4, 8, 128), F32)
                for c, mask in enumerate(masks(place, k, s)):
                    chosen = jnp.where(mask, cur_at[place, c], chosen)
                product = jnp.sum(got[place, k, s] * chosen, axis=0)
                lane_dots[k, place * CAP + s : place * CAP + s + 1, :] = jnp.sum(
                    product, axis=0, keepdims=True
                )

    def part_copy(way, hops, h):
        rows = slice(h * half, (h + 1) * half)
        return remote(
            part.at[way, hops - 1, rows],
            part_got.at[way, hops - 1, rows],
            part_s.at[way, hops - 1, h],
            part_r.at[way, hops - 1, h],
            at(dz=1 if way == 0 else NZ - 1),
        )

    part_copies = {
        (way, hops, h): part_copy(way, hops, h)
        for way in (0, 1)
        for hops in range(1, 5)
        for h in halves(hops, way)
    }

    def combine_ring(hops):
        if hops == 4:
            combine(PLACE[4], lambda c: part.at[c // half, 3, c])
        else:
            combine(PLACE[hops], lambda c: part.at[0, hops - 1, c])
            combine(PLACE[NZ - hops], lambda c: part.at[1, hops - 1, c])

    def pass_sums(hops):
        for h in (0, 1):
            for way in (0, 1):
                if h in halves(hops + 1, way):
                    part_copies[way, hops + 1, h].wait_recv()
                    for c in range(h * half, (h + 1) * half):
                        part[way, hops - 1, c] += part_got[way, hops, c]
                part_copies[way, hops, h].start()

    msgs = [
        remote(msg.at[k], msg_got.at[k], msg_s.at[k], msg_r.at[k], at(dx=k))
        for k in range(1, NX)
    ]
    for copy in msgs:
        copy.start()
    send_terms(0)
    send_terms(1)
    pass_currents(2, 0)
    send_terms(2)
    pass_currents(2, 1)
    send_terms(3)
    for copy in msgs:
        copy.wait_recv()
    arrive(PLACE[4])
    combine_ring(4)
    for way in (0, 1):
        part_copies[way, 4, way].start()
    pass_currents(3, 0)
    send_terms(4)
    pass_currents(3, 1)
    far_sum[...] = msg_got[0, 0:16] + msg_got[1, 0:16] + msg_got[2, 0:16] + msg_got[3, 0:16]
    fars = [
        remote(far_sum, far_got.at[k], far_s.at[k], far_r.at[k], at(dz=k)) for k in range(1, NZ)
    ]
    for copy in fars:
        copy.start()
    arrive(PLACE[3], PLACE[5])
    combine_ring(3)
    pass_sums(3)
    send_terms(5)
    pass_currents(4, 0)
    send_terms(6)
    pass_currents(4, 1)
    send_terms(7)
    arrive(PLACE[2], PLACE[6])
    arrive(PLACE[1], PLACE[7])
    dots(PLACE[1])
    dots(PLACE[7])
    dots(PLACE[2])
    dots(PLACE[6])
    dots(PLACE[3])
    dots(PLACE[5])
    for way in (0, 1):
        cur_copies[way, 4, way].wait_recv()
    dots(PLACE[4])
    arrive(PLACE[0])
    dots(PLACE[0])

    value = jnp.zeros((8, 128), F32)
    box_lane = lax.broadcasted_iota(jnp.int32, (NZ * CAP, 128), 1).astype(F32)
    for k in range(NX):
        rate = msg_got[k, 40:64, 0:1]
        box = msg_got[k, 40:64, 64:65]
        pair_value = rate * jnp.sum(lane_dots[k], axis=1, keepdims=True)
        table = jnp.where(box_lane == box, pair_value, 0.0)
        value += table[0:8] + table[8:16] + table[16:24]
    g_sum[0] = jnp.sum(value, axis=0, keepdims=True)

    g_all = [
        [
            remote(
                g_sum.at[stage],
                g_got.at[stage, place],
                g_s.at[stage, place],
                g_r.at[stage, place],
                device,
            )
            for place, device in groups[stage]
        ]
        for stage in range(3)
    ]

    def g_gather(stage):
        total = g_sum[stage]
        for (place, _), copy in zip(groups[stage], g_all[stage]):
            copy.wait_recv()
            total = total + g_got[stage, place]
        return total

    for copy in g_all[0]:
        copy.start()
    combine_ring(2)
    pass_sums(2)
    combine_ring(1)
    pass_sums(1)
    combine(PLACE[0], lambda c: own_sum.at[c])
    g_sum[1] = g_gather(0)
    for copy in g_all[1]:
        copy.start()

    for copy in fars:
        copy.wait_recv()
    far = far_sum[...]
    for k in range(1, NZ):
        far = far + far_got[k]
    far = far * norm_far
    far_re = jnp.broadcast_to(far[:, 0:1], (16, 128))
    far_im = jnp.broadcast_to(far[:, 64:65], (16, 128))

    def finish(h):
        for way in (0, 1):
            part_copies[way, 1, h].wait_recv()
        for c in range(h * half, (h + 1) * half):
            re = pl.ds(2 * c, 16, stride=16)
            im = pl.ds(2 * c + 1, 16, stride=16)
            rr, ri = rad[re, :], rad[im, :]
            total = (own_sum[c] + (part_got[0, 0, c] + part_got[1, 0, c])).reshape(32, 128)
            res_re = ((far_re * rr + far_im * ri) - total[0:16]).astype(BF16)
            res_im = ((far_im * rr - far_re * ri) - total[16:32]).astype(BF16)
            lhs[c, 0:16, 0:128] = res_re
            lhs[c, 0:16, 128:256] = res_im
            lhs[c, 16:32, 0:128] = res_im
            lhs[c, 16:32, 128:256] = -res_re
            update = jnp.dot(lhs[c], inv[c], preferred_element_type=F32)
            out[re, :] = adj[re, :] + update[0:16]
            out[im, :] = adj[im, :] + update[16:32]

    inv_in.wait()
    finish(0)
    g_sum[2] = g_gather(1)
    for copy in g_all[2]:
        copy.start()
    finish(1)
    for copy in msgs + fars + g_all[0] + g_all[1]:
        copy.wait_send()
    for copy in list(cur_copies.values()) + list(part_copies.values()):
        copy.wait_send()
    for place in (0, 1, 2, 3, 4, 5, 6, 7):
        terms_gone(place)
    total = g_gather(2)
    for i in range(BOX_DEV):
        mine = lane[0:1] == b * BOX_DEV + i
        grad[:, i : i + 1] = jnp.sum(jnp.where(mine, total, 0.0), axis=1, keepdims=True) * grad_norm

    for copy in g_all[2]:
        copy.wait_send()


def on_device(
    adjoint,
    currents,
    radiation,
    near_blocks,
    inverse_blocks,
    col_device,
    col_offset,
    box_of_block,
    pair_rate,
):
    angles_here, blocks, unknowns = adjoint.shape[1], adjoint.shape[2], adjoint.shape[4]
    near_count = near_blocks.shape[1]
    pairs = blocks * near_count
    ny, nc = lax.axis_size("angle"), lax.axis_size("pol")
    basis_count = lax.axis_size("basis")
    rows = angles_here * blocks * 2

    vmem = pl.BlockSpec(memory_space=pltpu.VMEM)
    dma = pltpu.SemaphoreType.DMA
    sizes = (
        ny,
        nc,
        1.0 / math.sqrt(blocks * basis_count * unknowns),
        -1.0 / math.sqrt(4 * unknowns * angles_here * ny * near_count),
    )
    out, grad = pl.pallas_call(
        functools.partial(kernel, sizes),
        out_shape=(
            jax.ShapeDtypeStruct((rows, unknowns), F32),
            jax.ShapeDtypeStruct((1, BOX_DEV), F32),
        ),
        in_specs=[pl.BlockSpec(memory_space=pltpu.HBM)] * 9,
        out_specs=(vmem, vmem),
        scratch_shapes=[
            pltpu.SMEM((blocks,), jnp.int32),
            pltpu.VMEM((blocks, near_count), jnp.int32),
            pltpu.VMEM((blocks, near_count), jnp.int32),
            pltpu.VMEM((blocks, near_count), F32),
            pltpu.VMEM((rows, unknowns), F32),
            pltpu.VMEM((rows, unknowns), F32),
            pltpu.VMEM((rows, unknowns), F32),
            pltpu.VMEM((pairs, 2 * unknowns, unknowns), BF16),
            pltpu.VMEM((blocks, 2 * unknowns, unknowns), BF16),
            pltpu.VMEM((8, 128), jnp.int32),
            pltpu.SMEM((8, 128), jnp.int32),
            pltpu.VMEM((blocks, 32, 256), BF16),
            pltpu.VMEM((NZ, NX - 1, CAP, 4, 8, 128), F32),
            pltpu.VMEM((NZ, NX, CAP, 4, 8, 128), F32),
            pltpu.VMEM((NZ, blocks, 4, 8, 128), F32),
            pltpu.VMEM((2, 4, blocks, 4, 8, 128), F32),
            pltpu.VMEM((2, 4, blocks, 4, 8, 128), F32),
            pltpu.VMEM((blocks, 4, 8, 128), F32),
            pltpu.VMEM((NX, 64, 128), F32),
            pltpu.VMEM((NX, 64, 128), F32),
            pltpu.VMEM((16, 128), F32),
            pltpu.VMEM((NZ, 16, 128), F32),
            pltpu.VMEM((NX, NZ * CAP, 128), F32),
            pltpu.VMEM((3, 1, 128), F32),
            pltpu.VMEM((3, 8, 1, 128), F32),
            dma((10,)),
            dma((NZ, NX - 1)),
            dma((NZ, NX - 1)),
            dma((2, 4, 2)),
            dma((2, 4, 2)),
            dma((2, 4, 2)),
            dma((2, 4, 2)),
            dma((NX,)),
            dma((NX,)),
            dma((NZ,)),
            dma((NZ,)),
            dma((3, 8)),
            dma((3, 8)),
        ],
        compiler_params=pltpu.CompilerParams(
            collective_id=0, has_side_effects=True, vmem_limit_bytes=40 << 20
        ),
        name="sweep",
    )(*[pltpu.with_memory_space_constraint(a, pltpu.HBM) for a in (
        box_of_block,
        col_device,
        col_offset,
        pair_rate,
        adjoint.reshape(rows, unknowns),
        currents.reshape(rows, unknowns),
        radiation.reshape(rows, unknowns),
        near_blocks.reshape(pairs, 2 * unknowns, unknowns),
        inverse_blocks.reshape(blocks, 2 * unknowns, unknowns),
    )])
    return (out.reshape(adjoint.shape), grad.reshape(BOX_DEV))


def solution(mesh):
    placed = (
        P("pol", "angle", "basis", None, None),
        P("pol", "angle", "basis", None, None),
        P("pol", "angle", "basis", None, None),
        P("basis", None, None, None, None),
        P("basis", None, None, None),
        P("basis", None),
        P("basis", None),
        P("basis"),
        P("basis", None),
    )
    return jax.shard_map(
        on_device,
        mesh=mesh,
        in_specs=placed,
        out_specs=(P("pol", "angle", "basis", None, None), P("basis")),
        check_vma=False,
    )
```
